32 devices in a mesh: grp: 4 (over z), vox: 8 (over y, x, core).
Axes of the slice: x: 2, y: 2, z: 4, core: 2. Of those that a mesh axis runs over, the one named last changes fastest.
Arguments:
- log_modulus: float32 [96, 65536], P('grp', 'vox'), may hold values from -3 to 3
- basis: bfloat16 [1024, 128], replicated, may hold values from -0.1875 to 0.1875
- sensitivity: bfloat16 [8192, 128], P('vox'), may hold values from -0.5 to 0.5
- obs_block: int32 [8192, 1], P('vox'), may hold values from 0 to 63; in each aligned block of 1024 rows (0 to 1023, 1024 to 2047, ...) at most 32 rows name the same one
- observed: float32 [8192], P('vox'), may hold values from -9 to 9
- noise_scale: float32 [8192], P('vox'), may hold values from 0.5 to 2
- perturbation: float32 [96, 8192], P('grp', 'vox'), may hold values from -6 to 6
Outputs:
- updated: float32 [96, 65536], P('grp', 'vox')
The draws below stay inside these ranges and needn't reach their ends.
Inputs may be any that keep to these rules, and one draw needn't show every extreme that they name: `obs_block`: among the observations of one index of vox (aligned blocks of 1024 rows), no voxel block is read by more than 32 of them, and in every draw some block is read by exactly 32.
All inputs are finite; a program needn't handle non-finite values.
Results may differ from the reference program's by a relative error of at most 0.011.
Values may be sent and summed in bfloat16 or wider, within the bound.
No kernel may reach another device: no remote copies, remote signals or barrier semaphores. Data moves between devices by JAX's collectives and lax.ppermute only.
A program may use at most 64 MiB of HBM per device.

```python
import math
import jax
import jax.numpy as jnp
import numpy as np
from jax import lax

J_DEV = 24
OBS_DEV = 1024
BV = 1024
F = 128
J = 96
NB = 64
NV = 65536
NO = 8192
CAPB = 32
N_GRP = 4


def steps_of(rng, dims, split, least, largest):
    loudness = 1.0
    for dim, shards_of in split:
        draws = jax.random.uniform(jax.random.fold_in(jax.random.fold_in(rng, 6), dim), (shards_of,), jnp.float32, least / len(split), largest / len(split))
        loudness = loudness * jnp.repeat(jnp.exp(draws), dims[dim] // shards_of).reshape((-1,) + (1,) * (len(dims) - 1 - dim))
    return loudness


def deal_out(own_key, own, number, rows, number_of, top, reach, lean):
    sequence = jax.random.permutation(own_key, number_of)
    packed, ordinary = load_shares(number_of, rows * top, reach, lean, True), load_shares(number_of, rows * top, reach, lean, False)
    places = jnp.arange(number_of)

    def named(lengths, offset_by):
        used = int((lengths > 0).sum())
        fixed = max(1, used // 4)
        shifted = fixed + (places - fixed + offset_by * (used - fixed)) % max(1, number_of - fixed)
        return jnp.zeros((number_of,), jnp.int32).at[sequence[jnp.where(places < fixed, places, shifted)]].set(jnp.asarray(lengths, jnp.int32))

    lengths = jnp.where(number % 4 == 0, named(packed, number // 4), named(ordinary, number - number // 4 - 1))
    mixed = jax.random.permutation(jax.random.fold_in(own, 3), number_of)
    giver, sink = mixed[0:number_of // 2 * 2:2], mixed[1:number_of // 2 * 2:2]
    room = jnp.minimum(lengths[giver] - 1, reach - lengths[sink]) // 2
    room = jnp.where((giver == sequence[0]) | (sink == sequence[0]) | (lengths[sink] == 0), 0, jnp.maximum(room, 0))
    shifted = jax.random.randint(jax.random.fold_in(own, 4), (number_of // 2,), 0, 1 << 20) % (room + 1)
    lengths = lengths.at[giver].add(-shifted).at[sink].add(shifted)
    items = jnp.searchsorted(jnp.cumsum(lengths), jnp.arange(rows * top), side="right").astype(jnp.int32)
    grid = items.reshape(top, rows).T
    grid = grid[jax.random.permutation(jax.random.fold_in(own, 1), rows)]
    offset_by = jax.random.randint(jax.random.fold_in(own, 2), (rows, 1), 0, top)
    return jnp.take_along_axis(grid, (jnp.arange(top)[None, :] + offset_by) % top, axis=1)


def load_shares(amount, total, reach, slope, full):
    weights = [(1 << 20) // math.isqrt(rank ** slope) + 1 for rank in range(1, amount + 1)]
    largest = reach if full else min(reach, max(-(-total // amount), total * weights[0] // sum(weights)))
    least = 1 if total - largest >= amount - 1 else 0
    counts, rest = [largest] + [least] * (amount - 1), total - largest - least * (amount - 1)
    while rest > 0:
        free = [i for i in range(1, amount) if counts[i] < largest] or [i for i in range(1, amount) if counts[i] < reach]
        mass, left = sum([weights[i] for i in free]), rest
        for i in free:
            more = min(reach - counts[i], max(1, left * weights[i] // mass), rest)
            counts[i] = counts[i] + more
            rest = rest - more
    return np.array(counts)


def centred(rng, dims, width, limit, pieces=(), kind=jnp.bfloat16):
    result = width * jax.random.normal(rng, dims, jnp.float32)
    if pieces:
        result = result * steps_of(rng, dims, pieces, -0.22, 0.18)
    return jnp.clip(result, -limit, limit).astype(kind)


def setup_inputs(seed: int = 0) -> dict:
    splits = jax.random.split(jax.random.key(seed), 8)
    log_modulus = centred(splits[0], (J, NV), 0.5, 3.0, ((0, 4), (1, 8)), jnp.float32)
    basis = centred(splits[1], (BV, F), BV ** -0.5, 0.1875)
    sensitivity = centred(splits[2], (NO, F), F ** -0.5, 0.5, ((0, 8),))
    obs_block_keys = jax.random.split(jax.random.fold_in(splits[3], 1), NO // OBS_DEV)
    obs_block_turns = jax.random.permutation(jax.random.fold_in(splits[3], 3), NO // OBS_DEV)
    obs_block = jax.vmap(lambda own, number: deal_out(jax.random.fold_in(splits[3], 2), own, number, OBS_DEV, NB, 1, CAPB, 1))(obs_block_keys, obs_block_turns).reshape((NO, 1))
    observed = centred(splits[4], (NO,), 1.5, 9.0, ((0, 8),), jnp.float32)
    noise_scale = jnp.clip(jnp.exp(math.log(2.0) - 1.3862944 * jax.random.uniform(splits[5], (NO,), jnp.float32) ** steps_of(splits[5], (NO,), ((0, 8),), -0.2, 0.2)), 0.5, 2.0)
    perturbation = centred(splits[6], (J, NO), 1.0, 6.0, ((0, 4), (1, 8)), jnp.float32)
    return {"log_modulus": log_modulus, "basis": basis, "sensitivity": sensitivity, "obs_block": obs_block, "observed": observed, "noise_scale": noise_scale, "perturbation": perturbation}


def reference(log_modulus, basis, sensitivity, obs_block, observed, noise_scale, perturbation):
    members = J_DEV * N_GRP
    compliance = jnp.exp(-log_modulus).astype(jnp.bfloat16)
    features = jnp.dot(compliance.reshape(members * NB, BV).astype(jnp.float32), basis.astype(jnp.float32), preferred_element_type=jnp.float32)
    features = features.astype(jnp.bfloat16).reshape(members, NB, F)
    blocks = obs_block[:, 0].astype(jnp.int32)
    sens_wide = sensitivity.astype(jnp.float32)

    def predict(member_feat):
        return lax.optimization_barrier(jnp.sum(sens_wide * member_feat[blocks].astype(jnp.float32), axis=1))
    predicted = lax.map(predict, features)
    scale_root = math.sqrt(members - 1)
    centre = lax.optimization_barrier(jnp.mean(predicted, axis=0))
    scaled = ((predicted - centre) / (noise_scale * scale_root)).astype(jnp.bfloat16)
    misfit = ((observed - predicted) / noise_scale + perturbation).astype(jnp.bfloat16)
    misfit_wide = misfit.astype(jnp.float32)
    damping = jnp.sum(misfit_wide * misfit_wide) / (members * NO)
    contract = (((1,), (1,)), ((), ()))
    gram_total = lax.dot_general(scaled.astype(jnp.float32), scaled.astype(jnp.float32), contract, preferred_element_type=jnp.float32)
    cross_total = lax.dot_general(scaled.astype(jnp.float32), misfit.astype(jnp.float32), contract, preferred_element_type=jnp.float32)
    system = gram_total + damping * jnp.eye(members, dtype=jnp.float32)
    factor = jnp.linalg.cholesky(system)
    halfway = lax.linalg.triangular_solve(factor, cross_total, left_side=True, lower=True)
    weights = lax.linalg.triangular_solve(factor, halfway, left_side=True, lower=True, transpose_a=True)
    weights_low = weights.astype(jnp.bfloat16)
    anomaly = log_modulus.astype(jnp.bfloat16)
    mixture = lax.dot_general(weights_low.astype(jnp.float32), anomaly.astype(jnp.float32), (((0,), (0,)), ((), ())), preferred_element_type=jnp.float32)
    return log_modulus + mixture / scale_root
```

```python
import functools
import math

import jax
import jax.numpy as jnp
from jax import lax
from jax.experimental import pallas as pl
from jax.experimental.pallas import tpu as pltpu
from jax.sharding import PartitionSpec as P

LANES = 128
SUBLANES = 8


def round_up(value, step):
    return -(-value // step) * step


def exchange(value, axis, distance):
    count = lax.axis_size(axis)
    return lax.ppermute(value, axis, [(i, i ^ distance) for i in range(count)])


def stages(count):
    bits = count.bit_length() - 1
    low, groups = 1, []
    while low < bits:
        width = min(2, bits - low)
        groups.append([step << low for step in range(1, 1 << width)])
        low += width
    return groups + ([[1]] if bits else [])


def gather_pieces(value, axis):
    stacks, offsets = [value], [[0]]
    for group in stages(lax.axis_size(axis)):
        whole = stacks[0] if len(stacks) == 1 else jnp.concatenate(stacks, axis=0)
        held = [offset for part in offsets for offset in part]
        stacks = [whole] + [exchange(whole, axis, distance) for distance in group]
        offsets = [held] + [[offset ^ distance for offset in held] for distance in group]
    return stacks, offsets


def predict_kernel(offsets, j_dev, blocks_dev, *refs):
    stack_refs = refs[: len(offsets)]
    sens_ref, key_ref, pert_ref, obs_ref, noise_ref, out_ref = refs[len(offsets) :]
    obs_dev = sens_ref.shape[0]
    rows = j_dev * blocks_dev
    tile = min(obs_dev, 2 * LANES)
    for start in range(0, obs_dev, tile):
        cols = pl.ds(start, tile)
        sens = sens_ref[cols, :]
        key = key_ref[:, cols]
        local = lax.broadcasted_iota(jnp.int32, (blocks_dev, tile), 0)
        total = jnp.zeros((j_dev, blocks_dev, tile), jnp.float32)
        for stack_ref, held in zip(stack_refs, offsets):
            for place, offset in enumerate(held):
                piece = stack_ref[pl.ds(place * rows, rows), :]
                product = lax.dot_general(
                    piece, sens, (((1,), (1,)), ((), ())), preferred_element_type=jnp.float32
                ).reshape(j_dev, blocks_dev, tile)
                wanted = (local + offset * blocks_dev == key)[None]
                total = total + jnp.where(wanted, product, 0.0)
        predicted = jnp.sum(total, axis=1)
        misfit = ((obs_ref[:, cols] - predicted) / noise_ref[:, cols] + pert_ref[:, cols]).astype(jnp.bfloat16)
        wide = misfit.astype(jnp.float32)
        out_ref[pl.ds(0, j_dev), cols] = predicted
        squares = jnp.sum(wide * wide, axis=0, keepdims=True)
        out_ref[pl.ds(j_dev, SUBLANES), cols] = jnp.broadcast_to(squares, (SUBLANES, tile))


def pair_kernel(groups, j_dev, scale_root, *refs):
    pred_refs = refs[:groups]
    pert_ref, obs_ref, noise_ref, out_ref = refs[groups:]
    members = groups * j_dev
    noise = noise_ref[...]
    own = pred_refs[0][pl.ds(0, j_dev), :]
    predicted = jnp.concatenate([ref[pl.ds(0, j_dev), :] for ref in pred_refs], axis=0)
    centre = jnp.sum(predicted, axis=0, keepdims=True) * (1.0 / members)
    scaled = ((predicted - centre) / (noise * scale_root)).astype(jnp.bfloat16)
    misfit = ((obs_ref[...] - own) / noise + pert_ref[...]).astype(jnp.bfloat16)
    contract = (((1,), (1,)), ((), ()))
    width = out_ref.shape[1]
    right = jnp.concatenate([scaled.astype(jnp.float32), misfit.astype(jnp.float32)], axis=0)
    pad = width - right.shape[0]
    if pad:
        right = jnp.concatenate([right, jnp.zeros((pad, right.shape[1]), jnp.float32)], axis=0)
    out_ref[pl.ds(0, members), :] = lax.dot_general(
        scaled, right.astype(jnp.bfloat16), contract, preferred_element_type=jnp.float32
    )
    squares = sum(ref[pl.ds(j_dev, 1), :] for ref in pred_refs)
    folded = sum(squares[:, at : at + width] for at in range(0, squares.shape[1], width))
    first = lax.broadcasted_iota(jnp.int32, (SUBLANES, width), 0) == 0
    out_ref[pl.ds(members, SUBLANES), :] = jnp.where(first, jnp.broadcast_to(folded, (SUBLANES, width)), 0.0)


def solve_kernel(members, right, count, *refs):
    part_refs, out_ref = refs[:-1], refs[-1]
    tile = (SUBLANES, LANES)
    groups = members // SUBLANES
    lane = lax.broadcasted_iota(jnp.int32, tile, 1)
    sub = lax.broadcasted_iota(jnp.int32, tile, 0)

    def load(group):
        rows = pl.ds(group * SUBLANES, SUBLANES)
        values = [ref[rows, :] for ref in part_refs]
        while len(values) > 1:
            values = [a + b for a, b in zip(values[::2], values[1::2])] + values[len(values) // 2 * 2 :]
        return values[0]

    damping = jnp.sum(load(groups), keepdims=True) * (1.0 / count)
    damping = jnp.broadcast_to(damping, tile)
    matrix = []
    for group in range(groups):
        matrix.append(load(group) + jnp.where(lane == sub + group * SUBLANES, damping, 0.0))

    def column(value, at):
        return jnp.broadcast_to(value[:, at : at + 1], tile)

    for block in range(groups):
        base = block * SUBLANES
        rows = [jnp.broadcast_to(matrix[block][i : i + 1, :], tile) for i in range(SUBLANES)]
        pivot = {(i, j): column(rows[i], base + j) for i in range(SUBLANES) for j in range(i, SUBLANES)}
        inverse = []
        for k in range(SUBLANES):
            inverse.append(1.0 / pivot[k, k])
            for i in range(k + 1, SUBLANES):
                factor = pivot[k, i] * inverse[k]
                for j in range(i, SUBLANES):
                    pivot[i, j] = pivot[i, j] - factor * pivot[k, j]
                rows[i] = rows[i] - factor * rows[k]
        for k in range(SUBLANES - 1, -1, -1):
            rows[k] = rows[k] * inverse[k]
            for i in range(k):
                rows[i] = rows[i] - pivot[i, k] * rows[k]
        for group in range(groups):
            if group == block:
                value = rows[0]
                for i in range(1, SUBLANES):
                    value = jnp.where(sub == i, rows[i], value)
            else:
                value = matrix[group]
                for i in range(SUBLANES):
                    value = value - column(matrix[group], base + i) * rows[i]
            matrix[group] = value
    for group in range(groups):
        out_ref[pl.ds(group * SUBLANES, SUBLANES), :] = matrix[group]


def solve_weights(parts, members, j_dev, count):
    if members + j_dev <= LANES and members % SUBLANES == 0:
        solved = pl.pallas_call(
            functools.partial(solve_kernel, members, j_dev, count),
            out_shape=jax.ShapeDtypeStruct((members, LANES), jnp.float32),
        )(*parts)
        return solved[:, members : members + j_dev]
    total = functools.reduce(jnp.add, parts)
    damping = jnp.sum(total[members:]) / count
    system = total[:members, :members] + damping * jnp.eye(members, dtype=jnp.float32)
    cross = total[:members, members : members + j_dev]
    factor = jnp.linalg.cholesky(system)
    halfway = lax.linalg.triangular_solve(factor, cross, left_side=True, lower=True)
    return lax.linalg.triangular_solve(factor, halfway, left_side=True, lower=True, transpose_a=True)


def on_device(log_modulus, basis, sensitivity, obs_block, observed, noise_scale, perturbation):
    n_vox = lax.axis_size("vox")
    n_grp = lax.axis_size("grp")
    j_dev, vox_dev = log_modulus.shape
    block_vox, feature_width = basis.shape
    blocks_dev = vox_dev // block_vox
    obs_dev = sensitivity.shape[0]
    members = j_dev * n_grp
    scale_root = math.sqrt(members - 1)

    low = log_modulus.astype(jnp.bfloat16)
    compliance = jnp.exp(-log_modulus).astype(jnp.bfloat16)
    features = jnp.dot(
        compliance.reshape(j_dev * blocks_dev, block_vox), basis, preferred_element_type=jnp.float32
    ).astype(jnp.bfloat16)

    blocks = obs_block[:, 0]
    key = ((blocks // blocks_dev) ^ lax.axis_index("vox")) * blocks_dev + blocks % blocks_dev
    key = key.reshape(1, obs_dev)
    observed = observed.reshape(1, obs_dev)
    noise = noise_scale.reshape(1, obs_dev)

    stacks, offsets = gather_pieces(features, "vox")
    payload = pl.pallas_call(
        functools.partial(predict_kernel, offsets, j_dev, blocks_dev),
        out_shape=jax.ShapeDtypeStruct((j_dev + SUBLANES, obs_dev), jnp.float32),
    )(*stacks, sensitivity, key, perturbation, observed, noise)
    payloads = [payload] + [exchange(payload, "grp", distance) for distance in range(1, n_grp)]
    width = round_up(members + j_dev, LANES)
    partial_sums = pl.pallas_call(
        functools.partial(pair_kernel, n_grp, j_dev, scale_root),
        out_shape=jax.ShapeDtypeStruct((members + SUBLANES, width), jnp.float32),
    )(*payloads, perturbation, observed, noise)
    parts = [partial_sums]
    for group in reversed(stages(n_vox)):
        total = functools.reduce(jnp.add, parts)
        parts = [total] + [exchange(total, "vox", distance) for distance in group]
    weights = solve_weights(parts, members, j_dev, members * obs_dev * n_vox)
    weights_low = weights.astype(jnp.bfloat16)

    anomalies = [low] + [exchange(low, "grp", distance) for distance in range(1, n_grp)]
    mixture = sum(
        lax.dot_general(
            weights_low[place * j_dev : (place + 1) * j_dev],
            anomaly,
            (((0,), (0,)), ((), ())),
            preferred_element_type=jnp.float32,
        )
        for place, anomaly in enumerate(anomalies)
    )
    return log_modulus + mixture / scale_root


def solution(mesh):
    in_specs = (
        P("grp", "vox"),
        P(),
        P("vox", None),
        P("vox", None),
        P("vox"),
        P("vox"),
        P("grp", "vox"),
    )
    out_specs = P("grp", "vox")
    return jax.shard_map(
        on_device, mesh=mesh, in_specs=in_specs, out_specs=out_specs, check_vma=False
    )
```

```python
import functools
import math

import jax
import jax.numpy as jnp
from jax import lax
from jax.experimental import pallas as pl
from jax.experimental.pallas import tpu as pltpu
from jax.sharding import PartitionSpec as P


LANES = 128
SUBLANES = 8


IN_VMEM = pl.BlockSpec(memory_space=pltpu.VMEM)
PIECE_ROWS = 32


def in_vmem(value):
    return pltpu.with_memory_space_constraint(value, pltpu.VMEM)


def in_hbm(value):
    return pltpu.with_memory_space_constraint(value, pltpu.HBM)


def vmem_call(kernel, outs, *operands):
    return pl.pallas_call(
        kernel,
        in_specs=[IN_VMEM] * len(operands),
        out_specs=[IN_VMEM] * len(outs),
        out_shape=[pltpu.VMEM(shape, dtype) for shape, dtype in outs],
    )(*map(in_vmem, operands))


def round_up(value, step):
    return -(-value // step) * step


def exchange(value, axis, distance):
    count = lax.axis_size(axis)
    return lax.ppermute(value, axis, [(i, i ^ distance) for i in range(count)])


def stages(count):
    bits = count.bit_length() - 1
    low, groups = 1, []
    while low < bits:
        width = min(2, bits - low)
        groups.append([step << low for step in range(1, 1 << width)])
        low += width
    return groups + ([[1]] if bits else [])


def gather_pieces(value, axis):
    stacks, offsets = [value], [[0]]
    for group in stages(lax.axis_size(axis)):
        whole = stacks[0] if len(stacks) == 1 else jnp.concatenate(stacks, axis=0)
        held = [offset for part in offsets for offset in part]
        stacks = [whole] + [exchange(whole, axis, distance) for distance in group]
        offsets = [held] + [[offset ^ distance for offset in held] for distance in group]
    return stacks, offsets


def two_parts(value):
    high = value.astype(jnp.bfloat16).astype(jnp.float32)
    return high, value - high


def predict_kernel(offsets, j_dev, blocks_dev, *refs):
    stack_refs = refs[: len(offsets)]
    sens_ref, block_ref, pert_ref, obs_ref, noise_ref, sent_ref, misfit_ref = refs[len(offsets) :]
    obs_dev = sens_ref.shape[0]
    rows = j_dev * blocks_dev
    tile = min(obs_dev, 2 * LANES)
    means, folded = [], jnp.zeros((1, LANES), jnp.float32)
    for start in range(0, obs_dev, tile):
        cols = pl.ds(start, tile)
        sens = sens_ref[cols, :]
        local = block_ref[:, cols] - lax.broadcasted_iota(jnp.int32, (blocks_dev, tile), 0)
        total = jnp.zeros((j_dev, blocks_dev, tile), jnp.float32)
        for stack_ref, held in zip(stack_refs, offsets):
            for place, offset in enumerate(held):
                piece = stack_ref[pl.ds(place * rows, rows), :]
                product = lax.dot_general(
                    piece, sens, (((1,), (1,)), ((), ())), preferred_element_type=jnp.float32
                ).reshape(j_dev, blocks_dev, tile)
                first_block = (lax.axis_index("vox") ^ offset) * blocks_dev
                total = total + jnp.where((local == first_block)[None], product, 0.0)
        predicted = jnp.sum(total, axis=1)
        misfit = ((obs_ref[:, cols] - predicted) / noise_ref[:, cols] + pert_ref[:, cols]).astype(jnp.bfloat16)
        misfit_ref[:, cols] = misfit
        mean = jnp.sum(predicted, axis=0, keepdims=True) * (1.0 / j_dev)
        sent_ref[:, cols] = (predicted - mean).astype(jnp.bfloat16)
        wide = misfit.astype(jnp.float32)
        squares = jnp.sum(wide * wide, axis=0, keepdims=True)
        for at in range(0, tile, LANES):
            means.append(mean[:, at : at + LANES])
            folded = folded + squares[:, at : at + LANES]
    mean_high, mean_low = two_parts(jnp.concatenate(means, axis=0))
    square_high, square_low = two_parts(folded)
    extra = [mean_high, mean_low, square_high, square_low]
    spare = j_dev - sum(part.shape[0] for part in extra)
    extra.append(jnp.zeros((spare, LANES), jnp.float32))
    sent_ref[:, pl.ds(obs_dev, LANES)] = jnp.concatenate(extra, axis=0).astype(jnp.bfloat16)


def pair_kernel(groups, j_dev, scale_root, *refs):
    sent_refs = refs[:groups]
    misfit_ref, noise_ref, out_ref = refs[groups:]
    members = groups * j_dev
    obs_dev = noise_ref.shape[1]
    strips = obs_dev // LANES
    means, squares = [], jnp.zeros((1, LANES), jnp.float32)
    for ref in sent_refs:
        extra = ref[:, pl.ds(obs_dev, LANES)].astype(jnp.float32)
        mean = extra[:strips] + extra[strips : 2 * strips]
        means.append(jnp.concatenate([mean[i : i + 1] for i in range(strips)], axis=1))
        squares = squares + extra[2 * strips : 2 * strips + 1] + extra[2 * strips + 1 : 2 * strips + 2]
    centre = sum(means) * (1.0 / groups)
    shrink = 1.0 / (noise_ref[...] * scale_root)
    scaled = jnp.concatenate(
        [
            (ref[:, pl.ds(0, obs_dev)].astype(jnp.float32) + (mean - centre)) * shrink
            for ref, mean in zip(sent_refs, means)
        ],
        axis=0,
    )
    width = out_ref.shape[1]
    right = [scaled, misfit_ref[...].astype(jnp.float32)]
    pad = width - members - j_dev
    if pad:
        right.append(jnp.zeros((pad, obs_dev), jnp.float32))
    out_ref[pl.ds(0, members), :] = lax.dot_general(
        scaled.astype(jnp.bfloat16),
        jnp.concatenate(right, axis=0).astype(jnp.bfloat16),
        (((1,), (1,)), ((), ())),
        preferred_element_type=jnp.float32,
    )
    first = lax.broadcasted_iota(jnp.int32, (SUBLANES, LANES), 0) == 0
    tail = jnp.where(first, jnp.broadcast_to(squares, (SUBLANES, LANES)), 0.0)
    if width > LANES:
        tail = jnp.concatenate([tail, jnp.zeros((SUBLANES, width - LANES), jnp.float32)], axis=1)
    out_ref[pl.ds(members, SUBLANES), :] = tail


def solve_turned(members, j_dev, count, part_refs):
    tile = (SUBLANES, LANES)
    groups = members // SUBLANES
    lane = lax.broadcasted_iota(jnp.int32, tile, 1)
    sub = lax.broadcasted_iota(jnp.int32, tile, 0)

    def load(group):
        rows = pl.ds(group * SUBLANES, SUBLANES)
        values = [ref[rows, :] for ref in part_refs]
        while len(values) > 1:
            values = [a + b for a, b in zip(values[::2], values[1::2])] + values[len(values) // 2 * 2 :]
        return values[0]

    damping = jnp.sum(load(groups), keepdims=True) * (1.0 / count)
    damping = jnp.broadcast_to(damping, tile)
    matrix = []
    for group in range(groups):
        matrix.append(load(group) + jnp.where(lane == sub + group * SUBLANES, damping, 0.0))

    def column(value, at):
        return jnp.broadcast_to(value[:, at : at + 1], tile)

    for block in range(groups):
        base = block * SUBLANES
        rows = [jnp.broadcast_to(matrix[block][i : i + 1, :], tile) for i in range(SUBLANES)]
        pivot = {(i, j): column(rows[i], base + j) for i in range(SUBLANES) for j in range(i, SUBLANES)}
        inverse = []
        for k in range(SUBLANES):
            inverse.append(1.0 / pivot[k, k])
            for i in range(k + 1, SUBLANES):
                factor = pivot[k, i] * inverse[k]
                for j in range(i, SUBLANES):
                    pivot[i, j] = pivot[i, j] - factor * pivot[k, j]
                rows[i] = rows[i] - factor * rows[k]
        for k in range(SUBLANES - 1, -1, -1):
            rows[k] = rows[k] * inverse[k]
            for i in range(k):
                rows[i] = rows[i] - pivot[i, k] * rows[k]
        for group in range(groups):
            if group == block:
                value = rows[0]
                for i in range(1, SUBLANES):
                    value = jnp.where(sub == i, rows[i], value)
            else:
                value = matrix[group]
                for i in range(SUBLANES):
                    value = value - column(matrix[group], base + i) * rows[i]
            matrix[group] = value
    padded = []
    for start in range(0, groups, j_dev // SUBLANES):
        padded += matrix[start : start + j_dev // SUBLANES]
        padded += [jnp.zeros(tile, jnp.float32)] * ((PIECE_ROWS - j_dev) // SUBLANES)
    padded += [jnp.zeros(tile, jnp.float32)] * (-len(padded) % (LANES // SUBLANES))
    turned = jnp.transpose(jnp.concatenate(padded, axis=0))
    return turned[members : members + j_dev, : members // j_dev * PIECE_ROWS].astype(jnp.bfloat16)


def solve_plain(parts, members, j_dev, count):
    total = functools.reduce(jnp.add, parts)
    damping = jnp.sum(total[members:]) / count
    system = total[:members, :members] + damping * jnp.eye(members, dtype=jnp.float32)
    cross = total[:members, members : members + j_dev]
    factor = jnp.linalg.cholesky(system)
    halfway = lax.linalg.triangular_solve(factor, cross, left_side=True, lower=True)
    weights = lax.linalg.triangular_solve(factor, halfway, left_side=True, lower=True, transpose_a=True)
    return weights.astype(jnp.bfloat16)


def mix(weights, anomalies):
    stack = []
    for anomaly in anomalies:
        stack += [anomaly, jnp.zeros((PIECE_ROWS - anomaly.shape[0], anomaly.shape[1]), jnp.bfloat16)]
    return lax.dot_general(
        weights, jnp.concatenate(stack, axis=0), (((1,), (0,)), ((), ())), preferred_element_type=jnp.float32
    )


def weigh_kernel(members, j_dev, count, scale_root, shares, parts, *refs):
    part_refs, refs = refs[:parts], refs[parts:]
    fetched = 1 + sum(shares)
    hbm_refs, (weights_ref, mixed_ref), refs = refs[:fetched], refs[fetched : fetched + 2], refs[fetched + 2 :]
    local_refs, semaphores = refs[:fetched], refs[fetched]
    fetches = [
        pltpu.make_async_copy(far, near, semaphores.at[number])
        for number, (far, near) in enumerate(zip(hbm_refs, local_refs))
    ]
    for fetch in fetches:
        fetch.start()
    weights = solve_turned(members, j_dev, count, part_refs)
    weights_ref[...] = weights
    for fetch in fetches:
        fetch.wait()
    log_ref, piece_refs = local_refs[0], local_refs[1:]
    vox_dev = mixed_ref.shape[1]
    tile = min(vox_dev, SUBLANES * LANES)
    for start in range(0, vox_dev, tile):
        cols = pl.ds(start, tile)
        own = log_ref[:, cols]
        anomalies, at = [own.astype(jnp.bfloat16)], 0
        for share in shares:
            anomalies.append(functools.reduce(jnp.add, [ref[:, cols] for ref in piece_refs[at : at + share]]))
            at += share
        mixed_ref[:, cols] = own + mix(weights, anomalies) * (1.0 / scale_root)


def finish_kernel(scale_root, weights_ref, mixed_ref, last_ref, out_hbm, out_ref, semaphores):
    vox_dev = mixed_ref.shape[1]
    tile = vox_dev // semaphores.shape[0]
    weights = weights_ref[...]
    weights = weights[:, weights.shape[1] - PIECE_ROWS :]
    copies = []
    for number in range(semaphores.shape[0]):
        cols = pl.ds(number * tile, tile)
        out_ref[:, cols] = mixed_ref[:, cols] + mix(weights, [last_ref[:, cols]]) * (1.0 / scale_root)
        copy = pltpu.make_async_copy(out_ref.at[:, cols], out_hbm.at[:, cols], semaphores.at[number])
        copy.start()
        copies.append(copy)
    for copy in copies:
        copy.wait()


def weigh(parts, log_modulus, pieces, members, count, scale_root):
    j_dev, vox_dev = log_modulus.shape
    flat = [piece for share in pieces for piece in share]
    return pl.pallas_call(
        functools.partial(
            weigh_kernel, members, j_dev, count, scale_root, [len(share) for share in pieces], len(parts)
        ),
        in_specs=[IN_VMEM] * len(parts) + [pl.BlockSpec(memory_space=pl.ANY)] * (1 + len(flat)),
        out_specs=[IN_VMEM] * 2,
        out_shape=[
            pltpu.VMEM((j_dev, members // j_dev * PIECE_ROWS), jnp.bfloat16),
            pltpu.VMEM((j_dev, vox_dev), jnp.float32),
        ],
        scratch_shapes=[pltpu.VMEM((j_dev, vox_dev), jnp.float32)]
        + [pltpu.VMEM((j_dev, vox_dev), jnp.bfloat16)] * len(flat)
        + [pltpu.SemaphoreType.DMA((1 + len(flat),))],
    )(*map(in_vmem, parts), log_modulus, *flat)


def finish(weights, mixed, last, scale_root):
    j_dev, vox_dev = mixed.shape
    return pl.pallas_call(
        functools.partial(finish_kernel, scale_root),
        in_specs=[IN_VMEM] * 3,
        out_specs=pl.BlockSpec(memory_space=pl.ANY),
        out_shape=jax.ShapeDtypeStruct((j_dev, vox_dev), jnp.float32),
        scratch_shapes=[
            pltpu.VMEM((j_dev, vox_dev), jnp.float32),
            pltpu.SemaphoreType.DMA((vox_dev // min(vox_dev, SUBLANES * LANES),)),
        ],
    )(*map(in_vmem, [weights, mixed, last]))


def pairs_exchange(value, axis, pairs):
    return lax.ppermute(value, axis, pairs)


def on_device(log_modulus, basis, sensitivity, obs_block, observed, noise_scale, perturbation):
    n_vox = lax.axis_size("vox")
    n_grp = lax.axis_size("grp")
    j_dev, vox_dev = log_modulus.shape
    block_vox, _ = basis.shape
    blocks_dev = vox_dev // block_vox
    obs_dev = sensitivity.shape[0]
    members = j_dev * n_grp
    scale_root = math.sqrt(members - 1)

    low = log_modulus.astype(jnp.bfloat16)
    compliance = jnp.exp(-log_modulus).astype(jnp.bfloat16)
    features = jnp.dot(
        compliance.reshape(j_dev * blocks_dev, block_vox), basis, preferred_element_type=jnp.float32
    ).astype(jnp.bfloat16)

    block = obs_block.reshape(1, obs_dev)
    observed = observed.reshape(1, obs_dev)
    noise = noise_scale.reshape(1, obs_dev)
    stacks, offsets = gather_pieces(features, "vox")
    line = n_grp == 4
    if line:
        near = in_hbm(exchange(low, "grp", 1))
        middle = in_hbm(pairs_exchange(low, "grp", [(1, 2), (2, 1)]))
    sent, misfit = vmem_call(
        functools.partial(predict_kernel, offsets, j_dev, blocks_dev),
        [((j_dev, obs_dev + LANES), jnp.bfloat16), ((j_dev, obs_dev), jnp.bfloat16)],
        *stacks,
        sensitivity,
        block,
        perturbation,
        observed,
        noise,
    )
    payloads = [sent] + [exchange(sent, "grp", distance) for distance in range(1, n_grp)]
    if line:
        ends = [(1, 0), (2, 3)]
        near_far = in_hbm(pairs_exchange(near, "grp", [(1, 2), (2, 1)]))
        middle_far = in_hbm(pairs_exchange(middle, "grp", ends))
    width = round_up(members + j_dev, LANES)
    (partial_sums,) = vmem_call(
        functools.partial(pair_kernel, n_grp, j_dev, scale_root),
        [((members + SUBLANES, width), jnp.float32)],
        *payloads,
        misfit,
        noise,
    )
    parts = [partial_sums]
    for group in reversed(stages(n_vox)):
        total = functools.reduce(jnp.add, parts)
        parts = [total] + [exchange(total, "vox", distance) for distance in group]
    count = members * obs_dev * n_vox
    if line:
        far = pairs_exchange(near_far, "grp", ends)
        weights, mixed = weigh(
            parts, log_modulus, [[near], [near_far, middle_far], [middle]], members, count, scale_root
        )
        return finish(weights, mixed, far, scale_root)
    weights = solve_plain(parts, members, j_dev, count)
    mixture = jnp.zeros_like(log_modulus)
    for distance in range(n_grp):
        anomaly = exchange(low, "grp", distance) if distance else low
        own_weights = weights[distance * j_dev : (distance + 1) * j_dev]
        mixture += lax.dot_general(
            own_weights, anomaly, (((0,), (0,)), ((), ())), preferred_element_type=jnp.float32
        )
    return log_modulus + mixture / scale_root


def solution(mesh):
    in_specs = (
        P("grp", "vox"),
        P(),
        P("vox", None),
        P("vox", None),
        P("vox"),
        P("vox"),
        P("grp", "vox"),
    )
    out_specs = P("grp", "vox")

    return jax.shard_map(on_device, mesh=mesh, in_specs=in_specs, out_specs=out_specs, check_vma=False)
```

```python
import functools
import math

import jax
import jax.numpy as jnp
from jax import lax
from jax.experimental import pallas as pl
from jax.experimental.pallas import tpu as pltpu
from jax.sharding import PartitionSpec as P


LANES = 128
SUBLANES = 8


IN_VMEM = pl.BlockSpec(memory_space=pltpu.VMEM)
PIECE_ROWS = 32


def in_vmem(value):
    return pltpu.with_memory_space_constraint(value, pltpu.VMEM)


def in_hbm(value):
    return pltpu.with_memory_space_constraint(value, pltpu.HBM)


def vmem_call(kernel, outs, *operands):
    return pl.pallas_call(
        kernel,
        in_specs=[IN_VMEM] * len(operands),
        out_specs=[IN_VMEM] * len(outs),
        out_shape=[pltpu.VMEM(shape, dtype) for shape, dtype in outs],
    )(*map(in_vmem, operands))


def round_up(value, step):
    return -(-value // step) * step


def exchange(value, axis, distance):
    count = lax.axis_size(axis)
    return lax.ppermute(value, axis, [(i, i ^ distance) for i in range(count)])


def stages(count):
    bits = count.bit_length() - 1
    low, groups = 1, []
    while low < bits:
        width = min(2, bits - low)
        groups.append([step << low for step in range(1, 1 << width)])
        low += width
    return groups + ([[1]] if bits else [])


def gather_pieces(value, axis):
    stacks, offsets = [value], [[0]]
    for group in stages(lax.axis_size(axis)):
        whole = stacks[0] if len(stacks) == 1 else jnp.concatenate(stacks, axis=0)
        held = [offset for part in offsets for offset in part]
        stacks = [whole] + [exchange(whole, axis, distance) for distance in group]
        offsets = [held] + [[offset ^ distance for offset in held] for distance in group]
    return stacks, offsets


def two_parts(value):
    high = value.astype(jnp.bfloat16).astype(jnp.float32)
    return high, value - high


def predict_kernel(offsets, j_dev, blocks_dev, *refs):
    stack_refs = refs[: len(offsets)]
    sens_ref, block_ref, pert_ref, obs_ref, noise_ref, sent_ref, misfit_ref = refs[len(offsets) :]
    obs_dev = sens_ref.shape[0]
    rows = j_dev * blocks_dev
    tile = min(obs_dev, 2 * LANES)
    means, folded = [], jnp.zeros((1, LANES), jnp.float32)
    for start in range(0, obs_dev, tile):
        cols = pl.ds(start, tile)
        sens = sens_ref[cols, :]
        local = block_ref[:, cols] - lax.broadcasted_iota(jnp.int32, (blocks_dev, tile), 0)
        total = jnp.zeros((j_dev, blocks_dev, tile), jnp.float32)
        for stack_ref, held in zip(stack_refs, offsets):
            for place, offset in enumerate(held):
                piece = stack_ref[pl.ds(place * rows, rows), :]
                product = lax.dot_general(
                    piece, sens, (((1,), (1,)), ((), ())), preferred_element_type=jnp.float32
                ).reshape(j_dev, blocks_dev, tile)
                first_block = (lax.axis_index("vox") ^ offset) * blocks_dev
                total = total + jnp.where((local == first_block)[None], product, 0.0)
        predicted = jnp.sum(total, axis=1)
        misfit = ((obs_ref[:, cols] - predicted) / noise_ref[:, cols] + pert_ref[:, cols]).astype(jnp.bfloat16)
        misfit_ref[:, cols] = misfit
        mean = jnp.sum(predicted, axis=0, keepdims=True) * (1.0 / j_dev)
        sent_ref[:, cols] = (predicted - mean).astype(jnp.bfloat16)
        wide = misfit.astype(jnp.float32)
        squares = jnp.sum(wide * wide, axis=0, keepdims=True)
        for at in range(0, tile, LANES):
            means.append(mean[:, at : at + LANES])
            folded = folded + squares[:, at : at + LANES]
    mean_high, mean_low = two_parts(jnp.concatenate(means, axis=0))
    square_high, square_low = two_parts(folded)
    extra = [mean_high, mean_low, square_high, square_low]
    spare = j_dev - sum(part.shape[0] for part in extra)
    extra.append(jnp.zeros((spare, LANES), jnp.float32))
    sent_ref[:, pl.ds(obs_dev, LANES)] = jnp.concatenate(extra, axis=0).astype(jnp.bfloat16)


def pair_kernel(groups, j_dev, scale_root, *refs):
    sent_refs = refs[:groups]
    misfit_ref, noise_ref, out_ref = refs[groups:]
    members = groups * j_dev
    obs_dev = noise_ref.shape[1]
    strips = obs_dev // LANES
    means, squares = [], jnp.zeros((1, LANES), jnp.float32)
    for ref in sent_refs:
        extra = ref[:, pl.ds(obs_dev, LANES)].astype(jnp.float32)
        mean = extra[:strips] + extra[strips : 2 * strips]
        means.append(jnp.concatenate([mean[i : i + 1] for i in range(strips)], axis=1))
        squares = squares + extra[2 * strips : 2 * strips + 1] + extra[2 * strips + 1 : 2 * strips + 2]
    centre = sum(means) * (1.0 / groups)
    shrink = 1.0 / (noise_ref[...] * scale_root)
    scaled = jnp.concatenate(
        [
            (ref[:, pl.ds(0, obs_dev)].astype(jnp.float32) + (mean - centre)) * shrink
            for ref, mean in zip(sent_refs, means)
        ],
        axis=0,
    )
    width = out_ref.shape[1]
    right = [scaled, misfit_ref[...].astype(jnp.float32)]
    pad = width - members - j_dev
    if pad:
        right.append(jnp.zeros((pad, obs_dev), jnp.float32))
    out_ref[pl.ds(0, members), :] = lax.dot_general(
        scaled.astype(jnp.bfloat16),
        jnp.concatenate(right, axis=0).astype(jnp.bfloat16),
        (((1,), (1,)), ((), ())),
        preferred_element_type=jnp.float32,
    )
    first = lax.broadcasted_iota(jnp.int32, (SUBLANES, LANES), 0) == 0
    tail = jnp.where(first, jnp.broadcast_to(squares, (SUBLANES, LANES)), 0.0)
    if width > LANES:
        tail = jnp.concatenate([tail, jnp.zeros((SUBLANES, width - LANES), jnp.float32)], axis=1)
    out_ref[pl.ds(members, SUBLANES), :] = tail


def solve_turned(members, j_dev, count, part_refs):
    tile = (SUBLANES, LANES)
    groups = members // SUBLANES
    lane = lax.broadcasted_iota(jnp.int32, tile, 1)
    sub = lax.broadcasted_iota(jnp.int32, tile, 0)

    def load(group):
        rows = pl.ds(group * SUBLANES, SUBLANES)
        values = [ref[rows, :] for ref in part_refs]
        while len(values) > 1:
            values = [a + b for a, b in zip(values[::2], values[1::2])] + values[len(values) // 2 * 2 :]
        return values[0]

    damping = jnp.sum(load(groups), keepdims=True) * (1.0 / count)
    damping = jnp.broadcast_to(damping, tile)
    matrix = []
    for group in range(groups):
        matrix.append(load(group) + jnp.where(lane == sub + group * SUBLANES, damping, 0.0))

    def column(value, at):
        return jnp.broadcast_to(value[:, at : at + 1], tile)

    for block in range(groups):
        base = block * SUBLANES
        rows = [jnp.broadcast_to(matrix[block][i : i + 1, :], tile) for i in range(SUBLANES)]
        pivot = {(i, j): column(rows[i], base + j) for i in range(SUBLANES) for j in range(i, SUBLANES)}
        inverse = []
        for k in range(SUBLANES):
            inverse.append(1.0 / pivot[k, k])
            for i in range(k + 1, SUBLANES):
                factor = pivot[k, i] * inverse[k]
                for j in range(i, SUBLANES):
                    pivot[i, j] = pivot[i, j] - factor * pivot[k, j]
                rows[i] = rows[i] - factor * rows[k]
        for k in range(SUBLANES - 1, -1, -1):
            rows[k] = rows[k] * inverse[k]
            for i in range(k):
                rows[i] = rows[i] - pivot[i, k] * rows[k]
        for group in range(groups):
            if group == block:
                value = rows[0]
                for i in range(1, SUBLANES):
                    value = jnp.where(sub == i, rows[i], value)
            else:
                value = matrix[group]
                for i in range(SUBLANES):
                    value = value - column(matrix[group], base + i) * rows[i]
            matrix[group] = value
    padded = []
    for start in range(0, groups, j_dev // SUBLANES):
        padded += matrix[start : start + j_dev // SUBLANES]
        padded += [jnp.zeros(tile, jnp.float32)] * ((PIECE_ROWS - j_dev) // SUBLANES)
    padded += [jnp.zeros(tile, jnp.float32)] * (-len(padded) % (LANES // SUBLANES))
    turned = jnp.transpose(jnp.concatenate(padded, axis=0))
    return turned[members : members + j_dev, : members // j_dev * PIECE_ROWS].astype(jnp.bfloat16)


def solve_plain(parts, members, j_dev, count):
    total = functools.reduce(jnp.add, parts)
    damping = jnp.sum(total[members:]) / count
    system = total[:members, :members] + damping * jnp.eye(members, dtype=jnp.float32)
    cross = total[:members, members : members + j_dev]
    factor = jnp.linalg.cholesky(system)
    halfway = lax.linalg.triangular_solve(factor, cross, left_side=True, lower=True)
    weights = lax.linalg.triangular_solve(factor, halfway, left_side=True, lower=True, transpose_a=True)
    return weights.astype(jnp.bfloat16)


def mix(weights, anomalies):
    stack = []
    for anomaly in anomalies:
        stack += [anomaly, jnp.zeros((PIECE_ROWS - anomaly.shape[0], anomaly.shape[1]), jnp.bfloat16)]
    return lax.dot_general(
        weights, jnp.concatenate(stack, axis=0), (((1,), (0,)), ((), ())), preferred_element_type=jnp.float32
    )


def weigh_kernel(members, j_dev, count, scale_root, shares, parts, *refs):
    part_refs, refs = refs[:parts], refs[parts:]
    given = 1 + sum(shares)
    fetched = len(refs) - given - 3
    held_refs, (weights_ref, mixed_ref), refs = refs[:given], refs[given : given + 2], refs[given + 2 :]
    hbm_refs, (local_refs, semaphores) = held_refs[:fetched], (list(refs[:fetched]), refs[fetched])
    fetches = [
        pltpu.make_async_copy(far, near, semaphores.at[number])
        for number, (far, near) in enumerate(zip(hbm_refs, local_refs))
    ]
    for fetch in fetches:
        fetch.start()
    weights = solve_turned(members, j_dev, count, part_refs)
    weights_ref[...] = weights
    for fetch in fetches:
        fetch.wait()
    local_refs += held_refs[fetched:]
    log_ref, piece_refs = local_refs[0], local_refs[1:]
    vox_dev = mixed_ref.shape[1]
    tile = min(vox_dev, SUBLANES * LANES)
    for start in range(0, vox_dev, tile):
        cols = pl.ds(start, tile)
        own = log_ref[:, cols]
        anomalies, at = [own.astype(jnp.bfloat16)], 0
        for share in shares:
            anomalies.append(functools.reduce(jnp.add, [ref[:, cols] for ref in piece_refs[at : at + share]]))
            at += share
        anomalies[2], anomalies[3] = anomalies[3], anomalies[2]
        mixed_ref[:, cols] = own + mix(weights, anomalies) * (1.0 / scale_root)


def finish_kernel(scale_root, weights_ref, mixed_ref, last_ref, out_hbm, out_ref, semaphores):
    vox_dev = mixed_ref.shape[1]
    tile = vox_dev // semaphores.shape[0]
    weights = weights_ref[...]
    weights = weights[:, weights.shape[1] - PIECE_ROWS :]
    copies = []
    for number in range(semaphores.shape[0]):
        cols = pl.ds(number * tile, tile)
        out_ref[:, cols] = mixed_ref[:, cols] + mix(weights, [last_ref[:, cols]]) * (1.0 / scale_root)
        copy = pltpu.make_async_copy(out_ref.at[:, cols], out_hbm.at[:, cols], semaphores.at[number])
        copy.start()
        copies.append(copy)
    for copy in copies:
        copy.wait()


def weigh(parts, log_modulus, pieces, members, count, scale_root):
    j_dev, vox_dev = log_modulus.shape
    flat = [piece for share in pieces for piece in share]
    return pl.pallas_call(
        functools.partial(
            weigh_kernel, members, j_dev, count, scale_root, [len(share) for share in pieces], len(parts)
        ),
        in_specs=[IN_VMEM] * len(parts) + [pl.BlockSpec(memory_space=pl.ANY)] * len(flat) + [IN_VMEM],
        out_specs=[IN_VMEM] * 2,
        out_shape=[
            pltpu.VMEM((j_dev, members // j_dev * PIECE_ROWS), jnp.bfloat16),
            pltpu.VMEM((j_dev, vox_dev), jnp.float32),
        ],
        scratch_shapes=[pltpu.VMEM((j_dev, vox_dev), jnp.float32)]
        + [pltpu.VMEM((j_dev, vox_dev), jnp.bfloat16)] * (len(flat) - 1)
        + [pltpu.SemaphoreType.DMA((len(flat),))],
    )(*map(in_vmem, parts), log_modulus, *flat[:-1], in_vmem(flat[-1]))


def finish(weights, mixed, last, scale_root):
    j_dev, vox_dev = mixed.shape
    return pl.pallas_call(
        functools.partial(finish_kernel, scale_root),
        in_specs=[IN_VMEM] * 3,
        out_specs=pl.BlockSpec(memory_space=pl.ANY),
        out_shape=jax.ShapeDtypeStruct((j_dev, vox_dev), jnp.float32),
        scratch_shapes=[
            pltpu.VMEM((j_dev, vox_dev), jnp.float32),
            pltpu.SemaphoreType.DMA((vox_dev // min(vox_dev, SUBLANES * LANES),)),
        ],
    )(*map(in_vmem, [weights, mixed, last]))


def pairs_exchange(value, axis, pairs):
    return lax.ppermute(value, axis, pairs)


def on_device(log_modulus, basis, sensitivity, obs_block, observed, noise_scale, perturbation):
    n_vox = lax.axis_size("vox")
    n_grp = lax.axis_size("grp")
    j_dev, vox_dev = log_modulus.shape
    block_vox, _ = basis.shape
    blocks_dev = vox_dev // block_vox
    obs_dev = sensitivity.shape[0]
    members = j_dev * n_grp
    scale_root = math.sqrt(members - 1)

    low = log_modulus.astype(jnp.bfloat16)
    compliance = jnp.exp(-log_modulus).astype(jnp.bfloat16)
    features = jnp.dot(
        compliance.reshape(j_dev * blocks_dev, block_vox), basis, preferred_element_type=jnp.float32
    ).astype(jnp.bfloat16)

    block = obs_block.reshape(1, obs_dev)
    observed = observed.reshape(1, obs_dev)
    noise = noise_scale.reshape(1, obs_dev)
    stacks, offsets = gather_pieces(features, "vox")
    line = n_grp == 4
    if line:
        near = in_hbm(exchange(low, "grp", 1))
        middle = in_hbm(pairs_exchange(low, "grp", [(1, 2), (2, 1)]))
    sent, misfit = vmem_call(
        functools.partial(predict_kernel, offsets, j_dev, blocks_dev),
        [((j_dev, obs_dev + LANES), jnp.bfloat16), ((j_dev, obs_dev), jnp.bfloat16)],
        *stacks,
        sensitivity,
        block,
        perturbation,
        observed,
        noise,
    )
    payloads = [sent] + [exchange(sent, "grp", distance) for distance in range(1, n_grp)]
    if line:
        ends = [(1, 0), (2, 3)]
        near_far = in_hbm(pairs_exchange(near, "grp", [(1, 2), (2, 1)]))
        middle_far = pairs_exchange(middle, "grp", ends)
    width = round_up(members + j_dev, LANES)
    (partial_sums,) = vmem_call(
        functools.partial(pair_kernel, n_grp, j_dev, scale_root),
        [((members + SUBLANES, width), jnp.float32)],
        *payloads,
        misfit,
        noise,
    )
    parts = [partial_sums]
    for group in reversed(stages(n_vox)):
        total = functools.reduce(jnp.add, parts)
        parts = [total] + [exchange(total, "vox", distance) for distance in group]
    count = members * obs_dev * n_vox
    if line:
        far = pairs_exchange(near_far, "grp", ends)
        weights, mixed = weigh(
            parts, log_modulus, [[near], [middle], [near_far, middle_far]], members, count, scale_root
        )
        return finish(weights, mixed, far, scale_root)
    weights = solve_plain(parts, members, j_dev, count)
    mixture = jnp.zeros_like(log_modulus)
    for distance in range(n_grp):
        anomaly = exchange(low, "grp", distance) if distance else low
        own_weights = weights[distance * j_dev : (distance + 1) * j_dev]
        mixture += lax.dot_general(
            own_weights, anomaly, (((0,), (0,)), ((), ())), preferred_element_type=jnp.float32
        )
    return log_modulus + mixture / scale_root


def solution(mesh):
    in_specs = (
        P("grp", "vox"),
        P(),
        P("vox", None),
        P("vox", None),
        P("vox"),
        P("vox"),
        P("grp", "vox"),
    )
    out_specs = P("grp", "vox")

    return jax.shard_map(on_device, mesh=mesh, in_specs=in_specs, out_specs=out_specs, check_vma=False)
```

```python
import functools
import math

import jax
import jax.numpy as jnp
from jax import lax
from jax.experimental import pallas as pl
from jax.experimental.pallas import tpu as pltpu
from jax.sharding import PartitionSpec as P


LANES = 128
BATCHES = 1
SUBLANES = 8


IN_VMEM = pl.BlockSpec(memory_space=pltpu.VMEM)
PIECE_ROWS = 32


def in_vmem(value):
    return pltpu.with_memory_space_constraint(value, pltpu.VMEM)


def in_hbm(value):
    return pltpu.with_memory_space_constraint(value, pltpu.HBM)


def vmem_call(kernel, outs, *operands):
    return pl.pallas_call(
        kernel,
        in_specs=[IN_VMEM] * len(operands),
        out_specs=[IN_VMEM] * len(outs),
        out_shape=[pltpu.VMEM(shape, dtype) for shape, dtype in outs],
    )(*map(in_vmem, operands))


def round_up(value, step):
    return -(-value // step) * step


def exchange(value, axis, distance):
    count = lax.axis_size(axis)
    return lax.ppermute(value, axis, [(i, i ^ distance) for i in range(count)])


def stages(count):
    bits = count.bit_length() - 1
    low, groups = 1, []
    while low < bits:
        width = min(2, bits - low)
        groups.append([step << low for step in range(1, 1 << width)])
        low += width
    return groups + ([[1]] if bits else [])


def gather_pieces(value, axis):
    stacks, offsets = [value], [[0]]
    for group in stages(lax.axis_size(axis)):
        whole = stacks[0] if len(stacks) == 1 else jnp.concatenate(stacks, axis=0)
        held = [offset for part in offsets for offset in part]
        stacks = [whole] + [exchange(whole, axis, distance) for distance in group]
        offsets = [held] + [[offset ^ distance for offset in held] for distance in group]
    return stacks, offsets


def two_parts(value):
    high = value.astype(jnp.bfloat16).astype(jnp.float32)
    return high, value - high


def feature_kernel(block_vox, log_hbm, basis_hbm, low_ref, feature_ref, log_ref, basis_ref, semaphores):
    j_dev, vox_dev = log_ref.shape
    blocks = vox_dev // block_vox
    fetches = []
    for block in range(blocks):
        cols = pl.ds(block * block_vox, block_vox)
        fetches.append(pltpu.make_async_copy(log_hbm.at[:, cols], log_ref.at[:, cols], semaphores.at[block]))
        fetches[-1].start()
    fetch_basis = pltpu.make_async_copy(basis_hbm, basis_ref, semaphores.at[blocks])
    fetch_basis.start()
    batch = max(1, blocks // BATCHES)
    for start in range(0, blocks, batch):
        compliance = []
        for block in range(start, min(blocks, start + batch)):
            fetches[block].wait()
            cols = pl.ds(block * block_vox, block_vox)
            value = log_ref[:, cols]
            low_ref[:, cols] = value.astype(jnp.bfloat16)
            compliance.append(jnp.exp(-value))
        if start == 0:
            fetch_basis.wait()
        rows = len(compliance) * j_dev
        feature_ref[pl.ds(start * j_dev, rows), :] = jnp.dot(
            jnp.concatenate(compliance, axis=0).astype(jnp.bfloat16),
            basis_ref[...],
            preferred_element_type=jnp.float32,
        ).astype(jnp.bfloat16)


def make_features(log_modulus, basis):
    j_dev, vox_dev = log_modulus.shape
    block_vox, feature_width = basis.shape
    blocks = vox_dev // block_vox
    return pl.pallas_call(
        functools.partial(feature_kernel, block_vox),
        in_specs=[pl.BlockSpec(memory_space=pl.ANY)] * 2,
        out_specs=[IN_VMEM] * 2,
        out_shape=[
            pltpu.VMEM((j_dev, vox_dev), jnp.bfloat16),
            pltpu.VMEM((blocks * j_dev, feature_width), jnp.bfloat16),
        ],
        scratch_shapes=[
            pltpu.VMEM((j_dev, vox_dev), jnp.float32),
            pltpu.VMEM(basis.shape, basis.dtype),
            pltpu.SemaphoreType.DMA((blocks + 1,)),
        ],
    )(log_modulus, basis)


def predict_kernel(offsets, j_dev, blocks_dev, *refs):
    stack_refs = refs[: len(offsets)]
    sens_ref, block_ref, pert_ref, obs_ref, noise_ref, sent_ref, misfit_ref = refs[len(offsets) :]
    obs_dev = sens_ref.shape[0]
    rows = j_dev * blocks_dev
    tile = min(obs_dev, 2 * LANES)
    means, folded = [], jnp.zeros((1, LANES), jnp.float32)
    for start in range(0, obs_dev, tile):
        cols = pl.ds(start, tile)
        sens = sens_ref[cols, :]
        block = block_ref[:, cols]
        total = jnp.zeros((j_dev, tile), jnp.float32)
        for stack_ref, held in zip(stack_refs, offsets):
            for place, offset in enumerate(held):
                piece = stack_ref[pl.ds(place * rows, rows), :]
                product = lax.dot_general(
                    piece, sens, (((1,), (1,)), ((), ())), preferred_element_type=jnp.float32
                )
                first_block = (lax.axis_index("vox") ^ offset) * blocks_dev
                for local in range(blocks_dev):
                    wanted = jnp.broadcast_to(block == first_block + local, total.shape)
                    total = jnp.where(wanted, product[local * j_dev : (local + 1) * j_dev], total)
        predicted = total
        misfit = ((obs_ref[:, cols] - predicted) / noise_ref[:, cols] + pert_ref[:, cols]).astype(jnp.bfloat16)
        misfit_ref[:, cols] = misfit
        mean = jnp.sum(predicted, axis=0, keepdims=True) * (1.0 / j_dev)
        sent_ref[:, cols] = (predicted - mean).astype(jnp.bfloat16)
        wide = misfit.astype(jnp.float32)
        squares = jnp.sum(wide * wide, axis=0, keepdims=True)
        for at in range(0, tile, LANES):
            means.append(mean[:, at : at + LANES])
            folded = folded + squares[:, at : at + LANES]
    mean_high, mean_low = two_parts(jnp.concatenate(means, axis=0))
    square_high, square_low = two_parts(folded)
    extra = [mean_high, mean_low, square_high, square_low]
    spare = j_dev - sum(part.shape[0] for part in extra)
    extra.append(jnp.zeros((spare, LANES), jnp.float32))
    sent_ref[:, pl.ds(obs_dev, LANES)] = jnp.concatenate(extra, axis=0).astype(jnp.bfloat16)


def pair_kernel(groups, j_dev, scale_root, *refs):
    sent_refs = refs[:groups]
    misfit_ref, noise_ref, out_ref = refs[groups:]
    members = groups * j_dev
    obs_dev = noise_ref.shape[1]
    strips = obs_dev // LANES
    means, squares = [], jnp.zeros((1, LANES), jnp.float32)
    for ref in sent_refs:
        extra = ref[:, pl.ds(obs_dev, LANES)].astype(jnp.float32)
        mean = extra[:strips] + extra[strips : 2 * strips]
        means.append(jnp.concatenate([mean[i : i + 1] for i in range(strips)], axis=1))
        squares = squares + extra[2 * strips : 2 * strips + 1] + extra[2 * strips + 1 : 2 * strips + 2]
    centre = sum(means) * (1.0 / groups)
    shrink = 1.0 / (noise_ref[...] * scale_root)
    scaled = jnp.concatenate(
        [
            (ref[:, pl.ds(0, obs_dev)].astype(jnp.float32) + (mean - centre)) * shrink
            for ref, mean in zip(sent_refs, means)
        ],
        axis=0,
    )
    width = out_ref.shape[1]
    right = [scaled, misfit_ref[...].astype(jnp.float32)]
    pad = width - members - j_dev
    if pad:
        right.append(jnp.zeros((pad, obs_dev), jnp.float32))
    out_ref[pl.ds(0, members), :] = lax.dot_general(
        scaled.astype(jnp.bfloat16),
        jnp.concatenate(right, axis=0).astype(jnp.bfloat16),
        (((1,), (1,)), ((), ())),
        preferred_element_type=jnp.float32,
    )
    first = lax.broadcasted_iota(jnp.int32, (SUBLANES, LANES), 0) == 0
    tail = jnp.where(first, jnp.broadcast_to(squares, (SUBLANES, LANES)), 0.0)
    if width > LANES:
        tail = jnp.concatenate([tail, jnp.zeros((SUBLANES, width - LANES), jnp.float32)], axis=1)
    out_ref[pl.ds(members, SUBLANES), :] = tail


def solve_turned(members, j_dev, count, part_refs):
    tile = (SUBLANES, LANES)
    groups = members // SUBLANES
    lane = lax.broadcasted_iota(jnp.int32, tile, 1)
    sub = lax.broadcasted_iota(jnp.int32, tile, 0)

    def load(group):
        rows = pl.ds(group * SUBLANES, SUBLANES)
        values = [ref[rows, :] for ref in part_refs]
        while len(values) > 1:
            values = [a + b for a, b in zip(values[::2], values[1::2])] + values[len(values) // 2 * 2 :]
        return values[0]

    damping = jnp.sum(load(groups), keepdims=True) * (1.0 / count)
    damping = jnp.broadcast_to(damping, tile)
    matrix = []
    for group in range(groups):
        matrix.append(load(group) + jnp.where(lane == sub + group * SUBLANES, damping, 0.0))

    def column(value, at):
        return jnp.broadcast_to(value[:, at : at + 1], tile)

    for block in range(groups):
        base = block * SUBLANES
        rows = [jnp.broadcast_to(matrix[block][i : i + 1, :], tile) for i in range(SUBLANES)]
        pivot = {(i, j): column(rows[i], base + j) for i in range(SUBLANES) for j in range(i, SUBLANES)}
        inverse = []
        for k in range(SUBLANES):
            inverse.append(1.0 / pivot[k, k])
            for i in range(k + 1, SUBLANES):
                factor = pivot[k, i] * inverse[k]
                for j in range(i, SUBLANES):
                    pivot[i, j] = pivot[i, j] - factor * pivot[k, j]
                rows[i] = rows[i] - factor * rows[k]
        for k in range(SUBLANES - 1, -1, -1):
            rows[k] = rows[k] * inverse[k]
            for i in range(k):
                rows[i] = rows[i] - pivot[i, k] * rows[k]
        for group in range(groups):
            if group == block:
                value = rows[0]
                for i in range(1, SUBLANES):
                    value = jnp.where(sub == i, rows[i], value)
            else:
                value = matrix[group]
                for i in range(SUBLANES):
                    value = value - column(matrix[group], base + i) * rows[i]
            matrix[group] = value
    padded = []
    for start in range(0, groups, j_dev // SUBLANES):
        padded += matrix[start : start + j_dev // SUBLANES]
        padded += [jnp.zeros(tile, jnp.float32)] * ((PIECE_ROWS - j_dev) // SUBLANES)
    padded += [jnp.zeros(tile, jnp.float32)] * (-len(padded) % (LANES // SUBLANES))
    turned = jnp.transpose(jnp.concatenate(padded, axis=0))
    return turned[members : members + j_dev, : members // j_dev * PIECE_ROWS].astype(jnp.bfloat16)


def solve_plain(parts, members, j_dev, count):
    total = functools.reduce(jnp.add, parts)
    damping = jnp.sum(total[members:]) / count
    system = total[:members, :members] + damping * jnp.eye(members, dtype=jnp.float32)
    cross = total[:members, members : members + j_dev]
    factor = jnp.linalg.cholesky(system)
    halfway = lax.linalg.triangular_solve(factor, cross, left_side=True, lower=True)
    weights = lax.linalg.triangular_solve(factor, halfway, left_side=True, lower=True, transpose_a=True)
    return weights.astype(jnp.bfloat16)


def mix(weights, anomalies):
    stack = []
    for anomaly in anomalies:
        stack += [anomaly, jnp.zeros((PIECE_ROWS - anomaly.shape[0], anomaly.shape[1]), jnp.bfloat16)]
    return lax.dot_general(
        weights, jnp.concatenate(stack, axis=0), (((1,), (0,)), ((), ())), preferred_element_type=jnp.float32
    )


def weigh_kernel(members, j_dev, count, scale_root, shares, parts, *refs):
    part_refs, refs = refs[:parts], refs[parts:]
    given = 1 + sum(shares)
    fetched = len(refs) - given - 3
    held_refs, (weights_ref, mixed_ref), refs = refs[:given], refs[given : given + 2], refs[given + 2 :]
    hbm_refs, (local_refs, semaphores) = held_refs[:fetched], (list(refs[:fetched]), refs[fetched])
    fetches = [
        pltpu.make_async_copy(far, near, semaphores.at[number])
        for number, (far, near) in enumerate(zip(hbm_refs, local_refs))
    ]
    for fetch in fetches:
        fetch.start()
    weights = solve_turned(members, j_dev, count, part_refs)
    weights_ref[...] = weights
    for fetch in fetches:
        fetch.wait()
    local_refs += held_refs[fetched:]
    log_ref, piece_refs = local_refs[0], local_refs[1:]
    vox_dev = mixed_ref.shape[1]
    tile = min(vox_dev, SUBLANES * LANES)
    for start in range(0, vox_dev, tile):
        cols = pl.ds(start, tile)
        own = log_ref[:, cols]
        anomalies, at = [own.astype(jnp.bfloat16)], 0
        for share in shares:
            anomalies.append(functools.reduce(jnp.add, [ref[:, cols] for ref in piece_refs[at : at + share]]))
            at += share
        anomalies[2], anomalies[3] = anomalies[3], anomalies[2]
        mixed_ref[:, cols] = own + mix(weights, anomalies) * (1.0 / scale_root)


def finish_kernel(scale_root, weights_ref, mixed_ref, last_ref, out_hbm, out_ref, semaphores):
    vox_dev = mixed_ref.shape[1]
    tile = vox_dev // semaphores.shape[0]
    weights = weights_ref[...]
    weights = weights[:, weights.shape[1] - PIECE_ROWS :]
    copies = []
    for number in range(semaphores.shape[0]):
        cols = pl.ds(number * tile, tile)
        out_ref[:, cols] = mixed_ref[:, cols] + mix(weights, [last_ref[:, cols]]) * (1.0 / scale_root)
        copy = pltpu.make_async_copy(out_ref.at[:, cols], out_hbm.at[:, cols], semaphores.at[number])
        copy.start()
        copies.append(copy)
    for copy in copies:
        copy.wait()


def weigh(parts, log_modulus, pieces, members, count, scale_root):
    j_dev, vox_dev = log_modulus.shape
    flat = [piece for share in pieces for piece in share]
    return pl.pallas_call(
        functools.partial(
            weigh_kernel, members, j_dev, count, scale_root, [len(share) for share in pieces], len(parts)
        ),
        in_specs=[IN_VMEM] * len(parts) + [pl.BlockSpec(memory_space=pl.ANY)] * len(flat) + [IN_VMEM],
        out_specs=[IN_VMEM] * 2,
        out_shape=[
            pltpu.VMEM((j_dev, members // j_dev * PIECE_ROWS), jnp.bfloat16),
            pltpu.VMEM((j_dev, vox_dev), jnp.float32),
        ],
        scratch_shapes=[pltpu.VMEM((j_dev, vox_dev), jnp.float32)]
        + [pltpu.VMEM((j_dev, vox_dev), jnp.bfloat16)] * (len(flat) - 1)
        + [pltpu.SemaphoreType.DMA((len(flat),))],
    )(*map(in_vmem, parts), log_modulus, *flat[:-1], in_vmem(flat[-1]))


def finish(weights, mixed, last, scale_root):
    j_dev, vox_dev = mixed.shape
    return pl.pallas_call(
        functools.partial(finish_kernel, scale_root),
        in_specs=[IN_VMEM] * 3,
        out_specs=pl.BlockSpec(memory_space=pl.ANY),
        out_shape=jax.ShapeDtypeStruct((j_dev, vox_dev), jnp.float32),
        scratch_shapes=[
            pltpu.VMEM((j_dev, vox_dev), jnp.float32),
            pltpu.SemaphoreType.DMA((vox_dev // min(vox_dev, SUBLANES * LANES),)),
        ],
    )(*map(in_vmem, [weights, mixed, last]))


def pairs_exchange(value, axis, pairs):
    return lax.ppermute(value, axis, pairs)


def on_device(log_modulus, basis, sensitivity, obs_block, observed, noise_scale, perturbation):
    n_vox = lax.axis_size("vox")
    n_grp = lax.axis_size("grp")
    j_dev, vox_dev = log_modulus.shape
    block_vox, _ = basis.shape
    blocks_dev = vox_dev // block_vox
    obs_dev = sensitivity.shape[0]
    members = j_dev * n_grp
    scale_root = math.sqrt(members - 1)

    low, features = make_features(log_modulus, basis)
    block = obs_block.reshape(1, obs_dev)
    observed = observed.reshape(1, obs_dev)
    noise = noise_scale.reshape(1, obs_dev)
    stacks, offsets = gather_pieces(features, "vox")
    line = n_grp == 4
    if line:
        near = in_hbm(exchange(low, "grp", 1))
        middle = in_hbm(pairs_exchange(low, "grp", [(1, 2), (2, 1)]))
    sent, misfit = vmem_call(
        functools.partial(predict_kernel, offsets, j_dev, blocks_dev),
        [((j_dev, obs_dev + LANES), jnp.bfloat16), ((j_dev, obs_dev), jnp.bfloat16)],
        *stacks,
        sensitivity,
        block,
        perturbation,
        observed,
        noise,
    )
    payloads = [sent] + [exchange(sent, "grp", distance) for distance in range(1, n_grp)]
    if line:
        ends = [(1, 0), (2, 3)]
        near_far = in_hbm(pairs_exchange(near, "grp", [(1, 2), (2, 1)]))
        middle_far = pairs_exchange(middle, "grp", ends)
    width = round_up(members + j_dev, LANES)
    (partial_sums,) = vmem_call(
        functools.partial(pair_kernel, n_grp, j_dev, scale_root),
        [((members + SUBLANES, width), jnp.float32)],
        *payloads,
        misfit,
        noise,
    )
    parts = [partial_sums]
    for group in reversed(stages(n_vox)):
        total = functools.reduce(jnp.add, parts)
        parts = [total] + [exchange(total, "vox", distance) for distance in group]
    count = members * obs_dev * n_vox
    if line:
        far = pairs_exchange(near_far, "grp", ends)
        weights, mixed = weigh(
            parts, log_modulus, [[near], [middle], [near_far, middle_far]], members, count, scale_root
        )
        return finish(weights, mixed, far, scale_root)
    weights = solve_plain(parts, members, j_dev, count)
    mixture = jnp.zeros_like(log_modulus)
    for distance in range(n_grp):
        anomaly = exchange(low, "grp", distance) if distance else low
        own_weights = weights[distance * j_dev : (distance + 1) * j_dev]
        mixture += lax.dot_general(
            own_weights, anomaly, (((0,), (0,)), ((), ())), preferred_element_type=jnp.float32
        )
    return log_modulus + mixture / scale_root


def solution(mesh):
    in_specs = (
        P("grp", "vox"),
        P(),
        P("vox", None),
        P("vox", None),
        P("vox"),
        P("vox"),
        P("grp", "vox"),
    )
    out_specs = P("grp", "vox")

    return jax.shard_map(on_device, mesh=mesh, in_specs=in_specs, out_specs=out_specs, check_vma=False)
```

```python
import functools
import math

import jax
import jax.numpy as jnp
from jax import lax
from jax.experimental import pallas as pl
from jax.experimental.pallas import tpu as pltpu
from jax.sharding import PartitionSpec as P


LANES = 128
BATCHES = 1
SUBLANES = 8


IN_VMEM = pl.BlockSpec(memory_space=pltpu.VMEM)
PIECE_ROWS = 32


def in_vmem(value):
    return pltpu.with_memory_space_constraint(value, pltpu.VMEM)


def in_hbm(value):
    return pltpu.with_memory_space_constraint(value, pltpu.HBM)


def vmem_call(kernel, outs, *operands):
    return pl.pallas_call(
        kernel,
        in_specs=[IN_VMEM] * len(operands),
        out_specs=[IN_VMEM] * len(outs),
        out_shape=[pltpu.VMEM(shape, dtype) for shape, dtype in outs],
    )(*map(in_vmem, operands))


def round_up(value, step):
    return -(-value // step) * step


def exchange(value, axis, distance):
    count = lax.axis_size(axis)
    return lax.ppermute(value, axis, [(i, i ^ distance) for i in range(count)])


def stages(count):
    bits = count.bit_length() - 1
    low, groups = 1, []
    while low < bits:
        width = min(2, bits - low)
        groups.append([step << low for step in range(1, 1 << width)])
        low += width
    return groups + ([[1]] if bits else [])


def gather_pieces(value, axis):
    stacks, offsets = [value], [[0]]
    for group in stages(lax.axis_size(axis)):
        whole = stacks[0] if len(stacks) == 1 else jnp.concatenate(stacks, axis=0)
        held = [offset for part in offsets for offset in part]
        stacks = [whole] + [exchange(whole, axis, distance) for distance in group]
        offsets = [held] + [[offset ^ distance for offset in held] for distance in group]
    return stacks, offsets


def two_parts(value):
    high = value.astype(jnp.bfloat16).astype(jnp.float32)
    return high, value - high


def feature_kernel(block_vox, log_hbm, basis_hbm, low_ref, feature_ref, log_ref, basis_ref, semaphores):
    j_dev, vox_dev = log_ref.shape
    blocks = vox_dev // block_vox
    fetches = []
    for block in range(blocks):
        cols = pl.ds(block * block_vox, block_vox)
        fetches.append(pltpu.make_async_copy(log_hbm.at[:, cols], log_ref.at[:, cols], semaphores.at[block]))
        fetches[-1].start()
    fetch_basis = pltpu.make_async_copy(basis_hbm, basis_ref, semaphores.at[blocks])
    fetch_basis.start()
    batch = max(1, blocks // BATCHES)
    for start in range(0, blocks, batch):
        compliance = []
        for block in range(start, min(blocks, start + batch)):
            fetches[block].wait()
            cols = pl.ds(block * block_vox, block_vox)
            value = log_ref[:, cols]
            low_ref[:, cols] = value.astype(jnp.bfloat16)
            compliance.append(jnp.exp(-value))
        if start == 0:
            fetch_basis.wait()
        rows = len(compliance) * j_dev
        feature_ref[pl.ds(start * j_dev, rows), :] = jnp.dot(
            jnp.concatenate(compliance, axis=0).astype(jnp.bfloat16),
            basis_ref[...],
            preferred_element_type=jnp.float32,
        ).astype(jnp.bfloat16)


def make_features(log_modulus, basis):
    j_dev, vox_dev = log_modulus.shape
    block_vox, feature_width = basis.shape
    blocks = vox_dev // block_vox
    return pl.pallas_call(
        functools.partial(feature_kernel, block_vox),
        in_specs=[pl.BlockSpec(memory_space=pl.ANY)] * 2,
        out_specs=[IN_VMEM] * 2,
        out_shape=[
            pltpu.VMEM((j_dev, vox_dev), jnp.bfloat16),
            pltpu.VMEM((blocks * j_dev, feature_width), jnp.bfloat16),
        ],
        scratch_shapes=[
            pltpu.VMEM((j_dev, vox_dev), jnp.float32),
            pltpu.VMEM(basis.shape, basis.dtype),
            pltpu.SemaphoreType.DMA((blocks + 1,)),
        ],
    )(log_modulus, basis)


def predict_kernel(offsets, j_dev, blocks_dev, *refs):
    stack_refs = refs[: len(offsets)]
    sens_ref, block_ref, pert_ref, obs_ref, noise_ref, sent_ref, misfit_ref = refs[len(offsets) :]
    obs_dev = sens_ref.shape[0]
    rows = j_dev * blocks_dev
    tile = min(obs_dev, 2 * LANES)
    means, folded = [], jnp.zeros((1, LANES), jnp.float32)
    for start in range(0, obs_dev, tile):
        cols = pl.ds(start, tile)
        sens = sens_ref[cols, :]
        block = block_ref[:, cols]
        total = jnp.zeros((j_dev, tile), jnp.float32)
        for stack_ref, held in zip(stack_refs, offsets):
            for place, offset in enumerate(held):
                piece = stack_ref[pl.ds(place * rows, rows), :]
                product = lax.dot_general(
                    piece, sens, (((1,), (1,)), ((), ())), preferred_element_type=jnp.float32
                )
                first_block = (lax.axis_index("vox") ^ offset) * blocks_dev
                for local in range(blocks_dev):
                    wanted = jnp.broadcast_to(block == first_block + local, total.shape)
                    total = jnp.where(wanted, product[local * j_dev : (local + 1) * j_dev], total)
        predicted = total
        misfit = ((obs_ref[:, cols] - predicted) / noise_ref[:, cols] + pert_ref[:, cols]).astype(jnp.bfloat16)
        misfit_ref[:, cols] = misfit
        mean = jnp.sum(predicted, axis=0, keepdims=True) * (1.0 / j_dev)
        sent_ref[:, cols] = (predicted - mean).astype(jnp.bfloat16)
        wide = misfit.astype(jnp.float32)
        squares = jnp.sum(wide * wide, axis=0, keepdims=True)
        for at in range(0, tile, LANES):
            means.append(mean[:, at : at + LANES])
            folded = folded + squares[:, at : at + LANES]
    mean_high, mean_low = two_parts(jnp.concatenate(means, axis=0))
    square_high, square_low = two_parts(folded)
    extra = [mean_high, mean_low, square_high, square_low]
    spare = j_dev - sum(part.shape[0] for part in extra)
    extra.append(jnp.zeros((spare, LANES), jnp.float32))
    sent_ref[:, pl.ds(obs_dev, LANES)] = jnp.concatenate(extra, axis=0).astype(jnp.bfloat16)


def pair_kernel(groups, j_dev, scale_root, *refs):
    sent_refs = refs[:groups]
    misfit_ref, noise_ref, out_ref = refs[groups:]
    members = groups * j_dev
    obs_dev = noise_ref.shape[1]
    strips = obs_dev // LANES
    means, squares = [], jnp.zeros((1, LANES), jnp.float32)
    for ref in sent_refs:
        extra = ref[:, pl.ds(obs_dev, LANES)].astype(jnp.float32)
        mean = extra[:strips] + extra[strips : 2 * strips]
        means.append(jnp.concatenate([mean[i : i + 1] for i in range(strips)], axis=1))
        squares = squares + extra[2 * strips : 2 * strips + 1] + extra[2 * strips + 1 : 2 * strips + 2]
    centre = sum(means) * (1.0 / groups)
    shrink = 1.0 / (noise_ref[...] * scale_root)
    scaled = jnp.concatenate(
        [
            (ref[:, pl.ds(0, obs_dev)].astype(jnp.float32) + (mean - centre)) * shrink
            for ref, mean in zip(sent_refs, means)
        ],
        axis=0,
    )
    width = out_ref.shape[1]
    right = [scaled, misfit_ref[...].astype(jnp.float32)]
    pad = width - members - j_dev
    if pad:
        right.append(jnp.zeros((pad, obs_dev), jnp.float32))
    out_ref[pl.ds(0, members), :] = lax.dot_general(
        scaled.astype(jnp.bfloat16),
        jnp.concatenate(right, axis=0).astype(jnp.bfloat16),
        (((1,), (1,)), ((), ())),
        preferred_element_type=jnp.float32,
    )
    first = lax.broadcasted_iota(jnp.int32, (SUBLANES, LANES), 0) == 0
    tail = jnp.where(first, jnp.broadcast_to(squares, (SUBLANES, LANES)), 0.0)
    if width > LANES:
        tail = jnp.concatenate([tail, jnp.zeros((SUBLANES, width - LANES), jnp.float32)], axis=1)
    out_ref[pl.ds(members, SUBLANES), :] = tail


def solve_turned(members, j_dev, count, part_refs):
    tile = (SUBLANES, LANES)
    groups = members // SUBLANES
    lane = lax.broadcasted_iota(jnp.int32, tile, 1)
    sub = lax.broadcasted_iota(jnp.int32, tile, 0)

    def load(group):
        rows = pl.ds(group * SUBLANES, SUBLANES)
        values = [ref[rows, :] for ref in part_refs]
        while len(values) > 1:
            values = [a + b for a, b in zip(values[::2], values[1::2])] + values[len(values) // 2 * 2 :]
        return values[0]

    damping = jnp.sum(load(groups), keepdims=True) * (1.0 / count)
    damping = jnp.broadcast_to(damping, tile)
    matrix = []
    for group in range(groups):
        matrix.append(load(group) + jnp.where(lane == sub + group * SUBLANES, damping, 0.0))

    def column(value, at):
        return jnp.broadcast_to(value[:, at : at + 1], tile)

    for block in range(groups):
        base = block * SUBLANES
        rows = [jnp.broadcast_to(matrix[block][i : i + 1, :], tile) for i in range(SUBLANES)]
        pivot = {(i, j): column(rows[i], base + j) for i in range(SUBLANES) for j in range(i, SUBLANES)}
        inverse = []
        for k in range(SUBLANES):
            inverse.append(1.0 / pivot[k, k])
            for i in range(k + 1, SUBLANES):
                factor = pivot[k, i] * inverse[k]
                for j in range(i, SUBLANES):
                    pivot[i, j] = pivot[i, j] - factor * pivot[k, j]
                rows[i] = rows[i] - factor * rows[k]
        for k in range(SUBLANES - 1, -1, -1):
            rows[k] = rows[k] * inverse[k]
            for i in range(k):
                rows[i] = rows[i] - pivot[i, k] * rows[k]
        for group in range(groups):
            if group == block:
                value = rows[0]
                for i in range(1, SUBLANES):
                    value = jnp.where(sub == i, rows[i], value)
            else:
                value = matrix[group]
                for i in range(SUBLANES):
                    value = value - column(matrix[group], base + i) * rows[i]
            matrix[group] = value
    padded = []
    for start in range(0, groups, j_dev // SUBLANES):
        padded += matrix[start : start + j_dev // SUBLANES]
        padded += [jnp.zeros(tile, jnp.float32)] * ((PIECE_ROWS - j_dev) // SUBLANES)
    padded += [jnp.zeros(tile, jnp.float32)] * (-len(padded) % (LANES // SUBLANES))
    turned = jnp.transpose(jnp.concatenate(padded, axis=0))
    return turned[members : members + j_dev, : members // j_dev * PIECE_ROWS].astype(jnp.bfloat16)


def solve_plain(parts, members, j_dev, count):
    total = functools.reduce(jnp.add, parts)
    damping = jnp.sum(total[members:]) / count
    system = total[:members, :members] + damping * jnp.eye(members, dtype=jnp.float32)
    cross = total[:members, members : members + j_dev]
    factor = jnp.linalg.cholesky(system)
    halfway = lax.linalg.triangular_solve(factor, cross, left_side=True, lower=True)
    weights = lax.linalg.triangular_solve(factor, halfway, left_side=True, lower=True, transpose_a=True)
    return weights.astype(jnp.bfloat16)


def mix(weights, anomalies):
    stack = []
    for anomaly in anomalies:
        stack += [anomaly, jnp.zeros((PIECE_ROWS - anomaly.shape[0], anomaly.shape[1]), jnp.bfloat16)]
    return lax.dot_general(
        weights, jnp.concatenate(stack, axis=0), (((1,), (0,)), ((), ())), preferred_element_type=jnp.float32
    )


def weigh_kernel(members, j_dev, count, scale_root, shares, parts, *refs):
    part_refs, refs = refs[:parts], refs[parts:]
    given = 1 + sum(shares)
    fetched = len(refs) - given - 3
    held_refs, (weights_ref, mixed_ref), refs = refs[:given], refs[given : given + 2], refs[given + 2 :]
    hbm_refs, (local_refs, semaphores) = held_refs[:fetched], (list(refs[:fetched]), refs[fetched])
    fetches = [
        pltpu.make_async_copy(far, near, semaphores.at[number])
        for number, (far, near) in enumerate(zip(hbm_refs, local_refs))
    ]
    for fetch in fetches:
        fetch.start()
    weights = solve_turned(members, j_dev, count, part_refs)
    weights_ref[...] = weights
    for fetch in fetches:
        fetch.wait()
    local_refs += held_refs[fetched:]
    log_ref, piece_refs = local_refs[0], local_refs[1:]
    vox_dev = mixed_ref.shape[1]
    tile = min(vox_dev, SUBLANES * LANES)
    for start in range(0, vox_dev, tile):
        cols = pl.ds(start, tile)
        own = log_ref[:, cols]
        anomalies, at = [own.astype(jnp.bfloat16)], 0
        for share in shares:
            anomalies.append(functools.reduce(jnp.add, [ref[:, cols] for ref in piece_refs[at : at + share]]))
            at += share
        anomalies[2], anomalies[3] = anomalies[3], anomalies[2]
        mixed_ref[:, cols] = own + mix(weights, anomalies) * (1.0 / scale_root)


def finish_kernel(scale_root, weights_ref, mixed_ref, last_ref, out_hbm, out_ref, semaphores):
    vox_dev = mixed_ref.shape[1]
    tile = vox_dev // semaphores.shape[0]
    weights = weights_ref[...]
    weights = weights[:, weights.shape[1] - PIECE_ROWS :]
    copies = []
    for number in range(semaphores.shape[0]):
        cols = pl.ds(number * tile, tile)
        out_ref[:, cols] = mixed_ref[:, cols] + mix(weights, [last_ref[:, cols]]) * (1.0 / scale_root)
        copy = pltpu.make_async_copy(out_ref.at[:, cols], out_hbm.at[:, cols], semaphores.at[number])
        copy.start()
        copies.append(copy)
    for copy in copies:
        copy.wait()


def weigh(parts, log_modulus, pieces, members, count, scale_root):
    j_dev, vox_dev = log_modulus.shape
    flat = [piece for share in pieces for piece in share]
    return pl.pallas_call(
        functools.partial(
            weigh_kernel, members, j_dev, count, scale_root, [len(share) for share in pieces], len(parts)
        ),
        in_specs=[IN_VMEM] * len(parts) + [pl.BlockSpec(memory_space=pl.ANY)] * len(flat) + [IN_VMEM],
        out_specs=[IN_VMEM] * 2,
        out_shape=[
            pltpu.VMEM((j_dev, members // j_dev * PIECE_ROWS), jnp.bfloat16),
            pltpu.VMEM((j_dev, vox_dev), jnp.float32),
        ],
        scratch_shapes=[pltpu.VMEM((j_dev, vox_dev), jnp.float32)]
        + [pltpu.VMEM((j_dev, vox_dev), jnp.bfloat16)] * (len(flat) - 1)
        + [pltpu.SemaphoreType.DMA((len(flat),))],
    )(*map(in_vmem, parts), log_modulus, *flat[:-1], in_vmem(flat[-1]))


def finish(weights, mixed, last, scale_root):
    j_dev, vox_dev = mixed.shape
    return pl.pallas_call(
        functools.partial(finish_kernel, scale_root),
        in_specs=[IN_VMEM] * 3,
        out_specs=pl.BlockSpec(memory_space=pl.ANY),
        out_shape=jax.ShapeDtypeStruct((j_dev, vox_dev), jnp.float32),
        scratch_shapes=[
            pltpu.VMEM((j_dev, vox_dev), jnp.float32),
            pltpu.SemaphoreType.DMA((vox_dev // min(vox_dev, SUBLANES * LANES),)),
        ],
    )(*map(in_vmem, [weights, mixed, last]))


def pairs_exchange(value, axis, pairs):
    return lax.ppermute(value, axis, pairs)


def on_device(log_modulus, basis, sensitivity, obs_block, observed, noise_scale, perturbation):
    n_vox = lax.axis_size("vox")
    n_grp = lax.axis_size("grp")
    j_dev, vox_dev = log_modulus.shape
    block_vox, _ = basis.shape
    blocks_dev = vox_dev // block_vox
    obs_dev = sensitivity.shape[0]
    members = j_dev * n_grp
    scale_root = math.sqrt(members - 1)

    low, features = make_features(log_modulus, basis)
    block = obs_block.reshape(1, obs_dev)
    observed = observed.reshape(1, obs_dev)
    noise = noise_scale.reshape(1, obs_dev)
    stacks, offsets = gather_pieces(features, "vox")
    line = n_grp == 4
    if line:
        near = in_hbm(exchange(low, "grp", 1))
        middle = in_hbm(pairs_exchange(low, "grp", [(1, 2), (2, 1)]))
    sent, misfit = vmem_call(
        functools.partial(predict_kernel, offsets, j_dev, blocks_dev),
        [((j_dev, obs_dev + LANES), jnp.bfloat16), ((j_dev, obs_dev), jnp.bfloat16)],
        *stacks,
        sensitivity,
        block,
        perturbation,
        observed,
        noise,
    )
    payloads = [sent] + [exchange(sent, "grp", distance) for distance in range(1, n_grp)]
    if line:
        near_far = in_hbm(pairs_exchange(near, "grp", [(1, 2), (2, 1)]))
        middle_far = exchange(middle, "grp", 1)
    width = round_up(members + j_dev, LANES)
    (partial_sums,) = vmem_call(
        functools.partial(pair_kernel, n_grp, j_dev, scale_root),
        [((members + SUBLANES, width), jnp.float32)],
        *payloads,
        misfit,
        noise,
    )
    parts = [partial_sums]
    for group in reversed(stages(n_vox)):
        total = functools.reduce(jnp.add, parts)
        parts = [total] + [exchange(total, "vox", distance) for distance in group]
    count = members * obs_dev * n_vox
    if line:
        far = exchange(near_far, "grp", 1)
        weights, mixed = weigh(
            parts, log_modulus, [[near], [middle], [near_far, middle_far]], members, count, scale_root
        )
        return finish(weights, mixed, far, scale_root)
    weights = solve_plain(parts, members, j_dev, count)
    mixture = jnp.zeros_like(log_modulus)
    for distance in range(n_grp):
        anomaly = exchange(low, "grp", distance) if distance else low
        own_weights = weights[distance * j_dev : (distance + 1) * j_dev]
        mixture += lax.dot_general(
            own_weights, anomaly, (((0,), (0,)), ((), ())), preferred_element_type=jnp.float32
        )
    return log_modulus + mixture / scale_root


def solution(mesh):
    in_specs = (
        P("grp", "vox"),
        P(),
        P("vox", None),
        P("vox", None),
        P("vox"),
        P("vox"),
        P("grp", "vox"),
    )
    out_specs = P("grp", "vox")

    return jax.shard_map(on_device, mesh=mesh, in_specs=in_specs, out_specs=out_specs, check_vma=False)
```

```python
import functools
import math

import jax
import jax.numpy as jnp
from jax import lax
from jax.experimental import pallas as pl
from jax.experimental.pallas import tpu as pltpu
from jax.sharding import PartitionSpec as P


LANES = 128
BATCHES = 1
SUBLANES = 8


IN_VMEM = pl.BlockSpec(memory_space=pltpu.VMEM)
PIECE_ROWS = 32


def in_vmem(value):
    return pltpu.with_memory_space_constraint(value, pltpu.VMEM)


def in_hbm(value):
    return pltpu.with_memory_space_constraint(value, pltpu.HBM)


def vmem_call(kernel, outs, *operands):
    return pl.pallas_call(
        kernel,
        in_specs=[IN_VMEM] * len(operands),
        out_specs=[IN_VMEM] * len(outs),
        out_shape=[pltpu.VMEM(shape, dtype) for shape, dtype in outs],
    )(*map(in_vmem, operands))


def round_up(value, step):
    return -(-value // step) * step


def exchange(value, axis, distance):
    count = lax.axis_size(axis)
    return lax.ppermute(value, axis, [(i, i ^ distance) for i in range(count)])


def stages(count):
    bits = count.bit_length() - 1
    low, groups = 1, []
    while low < bits:
        width = min(2, bits - low)
        groups.append([step << low for step in range(1, 1 << width)])
        low += width
    return groups + ([[1]] if bits else [])


def gather_pieces(value, axis):
    stacks, offsets = [value], [[0]]
    for group in stages(lax.axis_size(axis)):
        whole = stacks[0] if len(stacks) == 1 else jnp.concatenate(stacks, axis=0)
        held = [offset for part in offsets for offset in part]
        stacks = [whole] + [exchange(whole, axis, distance) for distance in group]
        offsets = [held] + [[offset ^ distance for offset in held] for distance in group]
    return stacks, offsets


def two_parts(value):
    high = value.astype(jnp.bfloat16).astype(jnp.float32)
    return high, value - high


def feature_kernel(block_vox, log_hbm, basis_hbm, low_ref, feature_ref, log_ref, basis_ref, semaphores):
    j_dev, vox_dev = log_ref.shape
    blocks = vox_dev // block_vox
    fetches = []
    for block in range(blocks):
        cols = pl.ds(block * block_vox, block_vox)
        fetches.append(pltpu.make_async_copy(log_hbm.at[:, cols], log_ref.at[:, cols], semaphores.at[block]))
        fetches[-1].start()
    fetch_basis = pltpu.make_async_copy(basis_hbm, basis_ref, semaphores.at[blocks])
    fetch_basis.start()
    batch = max(1, blocks // BATCHES)
    for start in range(0, blocks, batch):
        compliance = []
        for block in range(start, min(blocks, start + batch)):
            fetches[block].wait()
            cols = pl.ds(block * block_vox, block_vox)
            value = log_ref[:, cols]
            low_ref[:, cols] = value.astype(jnp.bfloat16)
            compliance.append(jnp.exp(-value))
        if start == 0:
            fetch_basis.wait()
        rows = len(compliance) * j_dev
        feature_ref[pl.ds(start * j_dev, rows), :] = jnp.dot(
            jnp.concatenate(compliance, axis=0).astype(jnp.bfloat16),
            basis_ref[...],
            preferred_element_type=jnp.float32,
        ).astype(jnp.bfloat16)


def make_features(log_modulus, basis):
    j_dev, vox_dev = log_modulus.shape
    block_vox, feature_width = basis.shape
    blocks = vox_dev // block_vox
    return pl.pallas_call(
        functools.partial(feature_kernel, block_vox),
        in_specs=[pl.BlockSpec(memory_space=pl.ANY)] * 2,
        out_specs=[IN_VMEM] * 2,
        out_shape=[
            pltpu.VMEM((j_dev, vox_dev), jnp.bfloat16),
            pltpu.VMEM((blocks * j_dev, feature_width), jnp.bfloat16),
        ],
        scratch_shapes=[
            pltpu.VMEM((j_dev, vox_dev), jnp.float32),
            pltpu.VMEM(basis.shape, basis.dtype),
            pltpu.SemaphoreType.DMA((blocks + 1,)),
        ],
    )(log_modulus, basis)


def predict_kernel(offsets, j_dev, blocks_dev, *refs):
    stack_refs = refs[: len(offsets)]
    sens_ref, block_ref, pert_ref, obs_ref, noise_ref, sent_ref, misfit_ref = refs[len(offsets) :]
    obs_dev = sens_ref.shape[0]
    rows = j_dev * blocks_dev
    tile = min(obs_dev, 2 * LANES)
    means, folded = [], jnp.zeros((1, LANES), jnp.float32)
    for start in range(0, obs_dev, tile):
        cols = pl.ds(start, tile)
        sens = sens_ref[cols, :]
        block = block_ref[:, cols]
        total = jnp.zeros((j_dev, tile), jnp.float32)
        for stack_ref, held in zip(stack_refs, offsets):
            for place, offset in enumerate(held):
                piece = stack_ref[pl.ds(place * rows, rows), :]
                product = lax.dot_general(
                    piece, sens, (((1,), (1,)), ((), ())), preferred_element_type=jnp.float32
                )
                first_block = (lax.axis_index("vox") ^ offset) * blocks_dev
                for local in range(blocks_dev):
                    wanted = jnp.broadcast_to(block == first_block + local, total.shape)
                    total = jnp.where(wanted, product[local * j_dev : (local + 1) * j_dev], total)
        predicted = total
        misfit = ((obs_ref[:, cols] - predicted) / noise_ref[:, cols] + pert_ref[:, cols]).astype(jnp.bfloat16)
        misfit_ref[:, cols] = misfit
        mean = jnp.sum(predicted, axis=0, keepdims=True) * (1.0 / j_dev)
        sent_ref[:, cols] = (predicted - mean).astype(jnp.bfloat16)
        wide = misfit.astype(jnp.float32)
        squares = jnp.sum(wide * wide, axis=0, keepdims=True)
        for at in range(0, tile, LANES):
            means.append(mean[:, at : at + LANES])
            folded = folded + squares[:, at : at + LANES]
    mean_high, mean_low = two_parts(jnp.concatenate(means, axis=0))
    square_high, square_low = two_parts(folded)
    extra = [mean_high, mean_low, square_high, square_low]
    spare = j_dev - sum(part.shape[0] for part in extra)
    extra.append(jnp.zeros((spare, LANES), jnp.float32))
    sent_ref[:, pl.ds(obs_dev, LANES)] = jnp.concatenate(extra, axis=0).astype(jnp.bfloat16)


def pair_kernel(groups, j_dev, scale_root, *refs):
    sent_refs = refs[:groups]
    misfit_ref, noise_ref, out_ref = refs[groups:]
    members = groups * j_dev
    obs_dev = noise_ref.shape[1]
    strips = obs_dev // LANES
    means, squares = [], jnp.zeros((1, LANES), jnp.float32)
    for ref in sent_refs:
        extra = ref[:, pl.ds(obs_dev, LANES)].astype(jnp.float32)
        mean = extra[:strips] + extra[strips : 2 * strips]
        means.append(jnp.concatenate([mean[i : i + 1] for i in range(strips)], axis=1))
        squares = squares + extra[2 * strips : 2 * strips + 1] + extra[2 * strips + 1 : 2 * strips + 2]
    centre = sum(means) * (1.0 / groups)
    shrink = 1.0 / (noise_ref[...] * scale_root)
    scaled = jnp.concatenate(
        [
            (ref[:, pl.ds(0, obs_dev)].astype(jnp.float32) + (mean - centre)) * shrink
            for ref, mean in zip(sent_refs, means)
        ],
        axis=0,
    )
    width = out_ref.shape[1]
    right = [scaled, misfit_ref[...].astype(jnp.float32)]
    pad = width - members - j_dev
    if pad:
        right.append(jnp.zeros((pad, obs_dev), jnp.float32))
    out_ref[pl.ds(0, members), :] = lax.dot_general(
        scaled.astype(jnp.bfloat16),
        jnp.concatenate(right, axis=0).astype(jnp.bfloat16),
        (((1,), (1,)), ((), ())),
        preferred_element_type=jnp.float32,
    )
    first = lax.broadcasted_iota(jnp.int32, (SUBLANES, LANES), 0) == 0
    tail = jnp.where(first, jnp.broadcast_to(squares, (SUBLANES, LANES)), 0.0)
    if width > LANES:
        tail = jnp.concatenate([tail, jnp.zeros((SUBLANES, width - LANES), jnp.float32)], axis=1)
    out_ref[pl.ds(members, SUBLANES), :] = tail


def solve_turned(members, j_dev, count, part_refs):
    tile = (SUBLANES, LANES)
    groups = members // SUBLANES
    lane = lax.broadcasted_iota(jnp.int32, tile, 1)
    sub = lax.broadcasted_iota(jnp.int32, tile, 0)

    def load(group):
        rows = pl.ds(group * SUBLANES, SUBLANES)
        values = [ref[rows, :] for ref in part_refs]
        while len(values) > 1:
            values = [a + b for a, b in zip(values[::2], values[1::2])] + values[len(values) // 2 * 2 :]
        return values[0]

    damping = jnp.sum(load(groups), keepdims=True) * (1.0 / count)
    damping = jnp.broadcast_to(damping, tile)
    matrix = []
    for group in range(groups):
        matrix.append(load(group) + jnp.where(lane == sub + group * SUBLANES, damping, 0.0))

    def column(value, at):
        return jnp.broadcast_to(value[:, at : at + 1], tile)

    for block in range(groups):
        base = block * SUBLANES
        rows = [jnp.broadcast_to(matrix[block][i : i + 1, :], tile) for i in range(SUBLANES)]
        pivot = {(i, j): column(rows[i], base + j) for i in range(SUBLANES) for j in range(i, SUBLANES)}
        inverse = []
        for k in range(SUBLANES):
            inverse.append(1.0 / pivot[k, k])
            for i in range(k + 1, SUBLANES):
                factor = pivot[k, i] * inverse[k]
                for j in range(i, SUBLANES):
                    pivot[i, j] = pivot[i, j] - factor * pivot[k, j]
                rows[i] = rows[i] - factor * rows[k]
        for k in range(SUBLANES - 1, -1, -1):
            rows[k] = rows[k] * inverse[k]
            for i in range(k):
                rows[i] = rows[i] - pivot[i, k] * rows[k]
        for group in range(groups):
            if group == block:
                value = rows[0]
                for i in range(1, SUBLANES):
                    value = jnp.where(sub == i, rows[i], value)
            else:
                value = matrix[group]
                for i in range(SUBLANES):
                    value = value - column(matrix[group], base + i) * rows[i]
            matrix[group] = value
    padded = []
    for start in range(0, groups, j_dev // SUBLANES):
        padded += matrix[start : start + j_dev // SUBLANES]
        padded += [jnp.zeros(tile, jnp.float32)] * ((PIECE_ROWS - j_dev) // SUBLANES)
    padded += [jnp.zeros(tile, jnp.float32)] * (-len(padded) % (LANES // SUBLANES))
    turned = jnp.transpose(jnp.concatenate(padded, axis=0))
    return turned[members : members + j_dev, : members // j_dev * PIECE_ROWS].astype(jnp.bfloat16)


def solve_plain(parts, members, j_dev, count):
    total = functools.reduce(jnp.add, parts)
    damping = jnp.sum(total[members:]) / count
    system = total[:members, :members] + damping * jnp.eye(members, dtype=jnp.float32)
    cross = total[:members, members : members + j_dev]
    factor = jnp.linalg.cholesky(system)
    halfway = lax.linalg.triangular_solve(factor, cross, left_side=True, lower=True)
    weights = lax.linalg.triangular_solve(factor, halfway, left_side=True, lower=True, transpose_a=True)
    return weights.astype(jnp.bfloat16)


def mix(weights, anomalies):
    stack = []
    for anomaly in anomalies:
        stack += [anomaly, jnp.zeros((PIECE_ROWS - anomaly.shape[0], anomaly.shape[1]), jnp.bfloat16)]
    return lax.dot_general(
        weights, jnp.concatenate(stack, axis=0), (((1,), (0,)), ((), ())), preferred_element_type=jnp.float32
    )


def weigh_kernel(members, j_dev, count, scale_root, shares, parts, *refs):
    part_refs, refs = refs[:parts], refs[parts:]
    given = 1 + sum(shares)
    fetched = len(refs) - given - 3
    held_refs, (weights_ref, mixed_ref), refs = refs[:given], refs[given : given + 2], refs[given + 2 :]
    hbm_refs, (local_refs, semaphores) = held_refs[:fetched], (list(refs[:fetched]), refs[fetched])
    fetches = [
        pltpu.make_async_copy(far, near, semaphores.at[number])
        for number, (far, near) in enumerate(zip(hbm_refs, local_refs))
    ]
    for fetch in fetches:
        fetch.start()
    weights = solve_turned(members, j_dev, count, part_refs)
    weights_ref[...] = weights
    for fetch in fetches:
        fetch.wait()
    local_refs += held_refs[fetched:]
    log_ref, piece_refs = local_refs[0], local_refs[1:]
    vox_dev = mixed_ref.shape[1]
    tile = min(vox_dev, SUBLANES * LANES)
    for start in range(0, vox_dev, tile):
        cols = pl.ds(start, tile)
        own = log_ref[:, cols]
        anomalies, at = [own.astype(jnp.bfloat16)], 0
        for share in shares:
            anomalies.append(functools.reduce(jnp.add, [ref[:, cols] for ref in piece_refs[at : at + share]]))
            at += share
        anomalies[2], anomalies[3] = anomalies[3], anomalies[2]
        mixed_ref[:, cols] = own + mix(weights, anomalies) * (1.0 / scale_root)


def finish_kernel(scale_root, weights_ref, mixed_ref, last_ref, out_hbm, out_ref, semaphores):
    vox_dev = mixed_ref.shape[1]
    tile = vox_dev // semaphores.shape[0]
    weights = weights_ref[...]
    weights = weights[:, weights.shape[1] - PIECE_ROWS :]
    copies = []
    for number in range(semaphores.shape[0]):
        cols = pl.ds(number * tile, tile)
        out_ref[:, cols] = mixed_ref[:, cols] + mix(weights, [last_ref[:, cols]]) * (1.0 / scale_root)
        copy = pltpu.make_async_copy(out_ref.at[:, cols], out_hbm.at[:, cols], semaphores.at[number])
        copy.start()
        copies.append(copy)
    for copy in copies:
        copy.wait()


def weigh(parts, log_modulus, pieces, members, count, scale_root):
    j_dev, vox_dev = log_modulus.shape
    flat = [piece for share in pieces for piece in share]
    return pl.pallas_call(
        functools.partial(
            weigh_kernel, members, j_dev, count, scale_root, [len(share) for share in pieces], len(parts)
        ),
        in_specs=[IN_VMEM] * len(parts) + [pl.BlockSpec(memory_space=pl.ANY)] * len(flat) + [IN_VMEM],
        out_specs=[IN_VMEM] * 2,
        out_shape=[
            pltpu.VMEM((j_dev, members // j_dev * PIECE_ROWS), jnp.bfloat16),
            pltpu.VMEM((j_dev, vox_dev), jnp.float32),
        ],
        scratch_shapes=[pltpu.VMEM((j_dev, vox_dev), jnp.float32)]
        + [pltpu.VMEM((j_dev, vox_dev), jnp.bfloat16)] * (len(flat) - 1)
        + [pltpu.SemaphoreType.DMA((len(flat),))],
    )(*map(in_vmem, parts), log_modulus, *flat[:-1], in_vmem(flat[-1]))


def finish(weights, mixed, last, scale_root):
    j_dev, vox_dev = mixed.shape
    return pl.pallas_call(
        functools.partial(finish_kernel, scale_root),
        in_specs=[IN_VMEM] * 3,
        out_specs=pl.BlockSpec(memory_space=pl.ANY),
        out_shape=jax.ShapeDtypeStruct((j_dev, vox_dev), jnp.float32),
        scratch_shapes=[
            pltpu.VMEM((j_dev, vox_dev), jnp.float32),
            pltpu.SemaphoreType.DMA((vox_dev // min(vox_dev, SUBLANES * LANES),)),
        ],
    )(*map(in_vmem, [weights, mixed, last]))


def pairs_exchange(value, axis, pairs):
    return lax.ppermute(value, axis, pairs)


def on_device(log_modulus, basis, sensitivity, obs_block, observed, noise_scale, perturbation):
    n_vox = lax.axis_size("vox")
    n_grp = lax.axis_size("grp")
    j_dev, vox_dev = log_modulus.shape
    block_vox, _ = basis.shape
    blocks_dev = vox_dev // block_vox
    obs_dev = sensitivity.shape[0]
    members = j_dev * n_grp
    scale_root = math.sqrt(members - 1)

    low, features = make_features(log_modulus, basis)
    block = obs_block.reshape(1, obs_dev)
    observed = observed.reshape(1, obs_dev)
    noise = noise_scale.reshape(1, obs_dev)
    stacks, offsets = gather_pieces(features, "vox")
    line = n_grp == 4
    if line:
        near = in_hbm(exchange(low, "grp", 1))
        middle = in_hbm(pairs_exchange(low, "grp", [(1, 2), (2, 1)]))
    sent, misfit = vmem_call(
        functools.partial(predict_kernel, offsets, j_dev, blocks_dev),
        [((j_dev, obs_dev + LANES), jnp.bfloat16), ((j_dev, obs_dev), jnp.bfloat16)],
        *stacks,
        sensitivity,
        block,
        perturbation,
        observed,
        noise,
    )
    payloads = [sent]
    for distance in range(1, n_grp):
        payloads.append(exchange(sent, "grp", distance))
    if line:
        near_far = in_hbm(pairs_exchange(near, "grp", [(1, 2), (2, 1)]))
        middle_far = exchange(middle, "grp", 1)
    width = round_up(members + j_dev, LANES)
    (partial_sums,) = vmem_call(
        functools.partial(pair_kernel, n_grp, j_dev, scale_root),
        [((members + SUBLANES, width), jnp.float32)],
        *payloads,
        misfit,
        noise,
    )
    parts = [partial_sums]
    for group in reversed(stages(n_vox)):
        total = functools.reduce(jnp.add, parts)
        parts = [total]
        for distance in group:
            parts.append(exchange(total, "vox", distance))
    count = members * obs_dev * n_vox
    if line:
        far = exchange(near_far, "grp", 1)
        weights, mixed = weigh(
            parts, log_modulus, [[near], [middle], [near_far, middle_far]], members, count, scale_root
        )
        return finish(weights, mixed, far, scale_root)
    weights = solve_plain(parts, members, j_dev, count)
    mixture = jnp.zeros_like(log_modulus)
    for distance in range(n_grp):
        anomaly = exchange(low, "grp", distance) if distance else low
        own_weights = weights[distance * j_dev : (distance + 1) * j_dev]
        mixture += lax.dot_general(
            own_weights, anomaly, (((0,), (0,)), ((), ())), preferred_element_type=jnp.float32
        )
    return log_modulus + mixture / scale_root


def solution(mesh):
    in_specs = (
        P("grp", "vox"),
        P(),
        P("vox", None),
        P("vox", None),
        P("vox"),
        P("vox"),
        P("grp", "vox"),
    )
    out_specs = P("grp", "vox")

    return jax.shard_map(on_device, mesh=mesh, in_specs=in_specs, out_specs=out_specs, check_vma=False)
```
